256 devices in a mesh: lon: 64 (over x_hi, z, y), lat: 4 (over x_lo, core).
Axes of the slice: x: 4 (x_hi: 2, x_lo: 2; x = x_hi * 2 + x_lo), y: 4, z: 8, core: 2. Of those that a mesh axis runs over, the one named last changes fastest.
Arguments:
- inputs: bfloat16 [32, 8192, 512], P('lat', 'lon'), may hold values from -16 to 16
- d_out: bfloat16 [32, 8192, 512], P('lat', 'lon'), may hold values from -6 to 6
- w_qkv: bfloat16 [512, 1536], replicated, may hold values from -0.25 to 0.25
- w_proj: bfloat16 [512, 512], replicated, may hold values from -0.25 to 0.25
- gain: float32 [512], replicated, may hold values from 0.1 to 1.9
- bias_table: float32 [465, 16], replicated, may hold values from -400 to 400
- rel_index: int32 [128, 128], replicated, may hold values from 0 to 464, as said below
- shifts: int32 [4], P('lat'), may hold values from 1 to 15, as said below
Outputs:
- d_inputs: bfloat16 [32, 8192, 512], P('lat', 'lon')
- g_qkv: float32 [512, 1536], P(('lon', 'lat'))
- g_proj: float32 [512, 512], P(('lon', 'lat'))
- g_gain: float32 [512], P(('lon', 'lat'))
- g_table: float32 [465, 16], replicated
The draws below stay inside these ranges and needn't reach their ends.
Inputs may be any that keep to these rules, and one draw needn't show every extreme that they name: `rel_index`: entry (i, j) depends only on the row and column offsets between window positions i and j, and distinct offsets give distinct entries. `shifts`: some band is shifted by 16 - 1.
All inputs are finite; a program needn't handle non-finite values.
Results may differ from the reference program's by a relative error of at most 0.0095.
Values may be sent and summed in bfloat16 or wider, within the bound.
A program may use at most 128 MiB of HBM per device.

```python
import jax
import jax.numpy as jnp
from jax import lax

C = 512
H = 16
HD = 32
WH = 8
WW = 16
WIN = 128
NREL = 465
LON_DEV = 128
LAT = 32
LON = 8192
TOKENS = 262144
N_LON = 64


def code_order(key):
    return jax.random.permutation(jax.random.fold_in(key, 11), NREL).astype(jnp.int32)


def draw_rel_index(key, part):
    codes = code_order(key)
    positions = jnp.arange(WIN, dtype=jnp.int32)
    row_pos = positions // WW
    col_pos = positions % WW
    offset = (row_pos[:, None] - row_pos[None, :] + WH - 1) * (2 * WW - 1) + (col_pos[:, None] - col_pos[None, :] + WW - 1)
    return codes[offset].astype(jnp.int32)


def draw_bias_table(key, part):
    drawn_draw = jax.random.normal(jax.random.fold_in(key, 23), (NREL, H), jnp.float32)
    return jnp.clip(drawn_draw, -4.0, 4.0)


def draw_shifts(key, part):
    count_rows = LAT // WH
    base_key = jax.random.fold_in(jax.random.fold_in(key, 43), part)
    values = jax.random.randint(jax.random.fold_in(base_key, 1), (count_rows,), 1, WW)
    chosen_row = jax.random.randint(jax.random.fold_in(base_key, 2), (), 0, count_rows)
    return values.at[chosen_row].set(WW - 1).astype(jnp.int32)


def strengthened(values, stream_key, source, target, shards_of, factor):
    owner, partner = [(jnp.arange(values.shape[dim]) // (values.shape[dim] // shards_of)).reshape([-1 if axis == dim else 1 for axis in range(values.ndim)]) for dim in (source, target)]
    chosen = jax.random.permutation(stream_key, shards_of)[partner]
    strong = (owner == chosen) | (owner == (partner + shards_of // 2) % shards_of)
    return jnp.where(strong, factor * values, values)


def levels(rng, extent, pieces, smallest, top_value):
    def one(position, shards_of):
        steps = jax.random.uniform(jax.random.fold_in(jax.random.fold_in(rng, 6), position), (shards_of,), jnp.float32, smallest / len(pieces), top_value / len(pieces))
        return jnp.repeat(jnp.exp(steps), extent[position] // shards_of).reshape((-1,) + (1,) * (len(extent) - position - 1))

    level = one(*pieces[0])
    for cut in pieces[1:]:
        level = level * one(*cut)
    return level


def gaussian(stream_key, extent, deviation, limit, pieces=(), kind=jnp.bfloat16):
    values = deviation * jax.random.normal(stream_key, extent, jnp.float32)
    if pieces:
        values = values * levels(stream_key, extent, pieces, -0.22, 0.18)
    return jnp.clip(values, -limit, limit).astype(kind)


def gaussian_with(rng, shape, deviation, reach, pieces, heavy, held_as=jnp.bfloat16):
    values = deviation * jax.random.normal(rng, shape, jnp.float32)
    if pieces:
        values = values * levels(rng, shape, pieces, -0.22, 0.18)
    return jnp.clip(strengthened(values, jax.random.fold_in(rng, 3), *heavy), -reach, reach).astype(held_as)


def setup_inputs(seed: int = 0) -> dict:
    key_list = jax.random.split(jax.random.key(seed), 9)
    return {
        "inputs": gaussian_with(key_list[0], (LAT, LON, C), 1.0, 16.0, ((0, 4), (1, 64)), (1, 2, 64, 4.0)),
        "d_out": gaussian(key_list[1], (LAT, LON, C), 1.0, 6.0, ((0, 4), (1, 64))),
        "w_qkv": gaussian(key_list[2], (C, 3 * C), C ** -0.5, 0.25),
        "w_proj": gaussian(key_list[3], (C, C), C ** -0.5, 0.25),
        "gain": jnp.clip(1.0 + 0.18 * jax.random.normal(key_list[4], (C,), jnp.float32), 0.1, 1.9),
        "bias_table": draw_bias_table(jax.random.fold_in(key_list[8], 71), 0),
        "rel_index": draw_rel_index(jax.random.fold_in(key_list[8], 71), 0),
        "shifts": draw_shifts(jax.random.fold_in(key_list[8], 71), 0),
    }


EPSILON = 1e-05

def rounded(value):
    return lax.optimization_barrier(value.astype(jnp.bfloat16)).astype(jnp.float32)

def to_windows(slab_field):
    span_count = slab_field.shape[1] // WW
    return slab_field.reshape(WH, span_count, WW, C).transpose(1, 0, 2, 3).reshape(span_count, WIN, C)

def from_windows(blocks, columns):
    span_count = columns // WW
    return blocks.reshape(span_count, WH, WW, C).transpose(1, 0, 2, 3).reshape(WH, columns, C)

def window_backward(inputs, d_out, w_qkv, w_proj, gain, bias_heads):
    number = inputs.shape[0]
    source = inputs.astype(jnp.float32)
    centred = source - lax.optimization_barrier(jnp.mean(source, axis=-1, keepdims=True))
    inv_std = lax.rsqrt(lax.optimization_barrier(jnp.mean(centred * centred, axis=-1, keepdims=True)) + EPSILON)
    normal_x = centred * inv_std
    normed = (normal_x * gain).astype(jnp.bfloat16).reshape(number * WIN, C)
    projected = rounded(jnp.dot(normed, w_qkv, preferred_element_type=jnp.float32))
    projected = projected.reshape(number, WIN, 3, H, HD)
    queries = projected[:, :, 0]
    key_heads = projected[:, :, 1]
    value_heads = projected[:, :, 2]
    factor = HD ** (-0.5)
    scores = jnp.einsum('nihd,njhd->nhij', queries, key_heads) * factor + bias_heads
    summit = lax.optimization_barrier(jnp.max(scores, axis=-1, keepdims=True))
    raised = jnp.exp(scores - summit)
    attention = raised / lax.optimization_barrier(jnp.sum(raised, axis=-1, keepdims=True))
    soft_low = rounded(attention)
    attended = jnp.einsum('nhij,njhd->nihd', soft_low, value_heads).astype(jnp.bfloat16)
    attended = attended.reshape(number * WIN, C)
    grad_rows = d_out.reshape(number * WIN, C)
    d_heads = rounded(jnp.dot(grad_rows, w_proj.T, preferred_element_type=jnp.float32))
    d_heads = d_heads.reshape(number, WIN, H, HD)
    term_proj = jnp.dot(attended.T, grad_rows, preferred_element_type=jnp.float32)
    d_soft = jnp.einsum('nihd,njhd->nhij', d_heads, value_heads)
    d_value = jnp.einsum('nhij,nihd->njhd', soft_low, d_heads)
    d_scores = attention * (d_soft - lax.optimization_barrier(jnp.sum(attention * d_soft, axis=-1, keepdims=True)))
    d_scores_low = rounded(d_scores)
    d_query = jnp.einsum('nhij,njhd->nihd', d_scores_low, key_heads) * factor
    d_key = jnp.einsum('nhij,nihd->njhd', d_scores_low, queries) * factor
    d_projected = jnp.stack([d_query, d_key, d_value], axis=2).astype(jnp.bfloat16)
    d_projected = d_projected.reshape(number * WIN, 3 * C)
    term_qkv = jnp.dot(normed.T, d_projected, preferred_element_type=jnp.float32)
    d_normed = jnp.dot(d_projected, w_qkv.T, preferred_element_type=jnp.float32).reshape(number, WIN, C)
    term_gain = lax.optimization_barrier(jnp.sum(d_normed * normal_x, axis=(0, 1)))
    scaled = d_normed * gain
    d_branch = inv_std * (scaled - lax.optimization_barrier(jnp.mean(scaled, axis=-1, keepdims=True)) - normal_x * lax.optimization_barrier(jnp.mean(scaled * normal_x, axis=-1, keepdims=True)))
    d_inputs = (d_out.astype(jnp.float32) + d_branch).astype(jnp.bfloat16)
    return (d_inputs, term_qkv, term_proj, term_gain, lax.optimization_barrier(jnp.sum(d_scores, axis=0)))

def reference(inputs, d_out, w_qkv, w_proj, gain, bias_table, rel_index, shifts):
    bias_heads = jnp.transpose(bias_table[rel_index], (2, 0, 1))
    band_count = LAT // WH
    per_block = LON_DEV // WW

    def block_step(running, block_pair):
        result = window_backward(block_pair[0], block_pair[1], w_qkv, w_proj, gain, bias_heads)
        summed = (running[0] + result[1], running[1] + result[2], running[2] + result[3], running[3] + result[4])
        return (summed, result[0])

    def row_step(running, band_item):
        input_band, grad_band, band_shift = band_item
        moved_x = jnp.roll(input_band, band_shift, axis=1)
        moved_d = jnp.roll(grad_band, band_shift, axis=1)
        blocks_x = to_windows(moved_x).reshape(N_LON, per_block, WIN, C)
        blocks_d = to_windows(moved_d).reshape(N_LON, per_block, WIN, C)
        running, d_blocks = lax.scan(block_step, running, (blocks_x, blocks_d))
        d_band = from_windows(d_blocks.reshape(N_LON * per_block, WIN, C), LON)
        return (running, jnp.roll(d_band, -band_shift, axis=1))
    start = (jnp.zeros((C, 3 * C), jnp.float32), jnp.zeros((C, C), jnp.float32), jnp.zeros((C,), jnp.float32), jnp.zeros((H, WIN, WIN), jnp.float32))
    running, d_bands = lax.scan(row_step, start, (inputs.reshape(band_count, WH, LON, C), d_out.reshape(band_count, WH, LON, C), shifts))
    d_inputs = d_bands.reshape(LAT, LON, C)
    grad_scale = TOKENS ** (-0.5)
    table_term = jax.ops.segment_sum(running[3].reshape(H, WIN * WIN).T, rel_index.reshape(WIN * WIN), num_segments=NREL)
    g_table = table_term * (TOKENS // WIN) ** (-0.5)
    return (d_inputs, running[0] * grad_scale, running[1] * grad_scale, running[2] * grad_scale, g_table)
```

```python
import functools

import jax
import jax.numpy as jnp
from jax import lax
from jax.experimental import pallas as pl
from jax.experimental.pallas import tpu as pltpu
from jax.sharding import PartitionSpec as P

C = 512
H = 16
HD = 32
WH = 8
WW = 16
WIN = 128
NREL = 465
COLS = 128
NWIN = 8
GROUPS = 4
TOK = NWIN * WIN
EPSILON = 1e-05
LOG2E = 1.4426950408889634
F32 = jnp.float32
BF16 = jnp.bfloat16

NN = (((1,), (0,)), ((), ()))
NT = (((1,), (1,)), ((), ()))


def mm(a, b, dims=NN):
    return lax.dot_general(a, b, dims, preferred_element_type=F32)


def iota(shape, dim):
    return lax.broadcasted_iota(jnp.int32, shape, dim)


def one_hot(cond):
    return jnp.where(cond, 1.0, 0.0).astype(BF16)


def split3(x):
    hi = x.astype(BF16)
    rest = x - hi.astype(F32)
    mid = rest.astype(BF16)
    low = (rest - mid.astype(F32)).astype(BF16)
    return hi, mid, low


def pair_masks(j):
    k = iota((WIN, WIN), 1)
    carry = (j % WW + k % WW) >= WW
    wrap = (j // WW + k // WW + carry.astype(jnp.int32)) >= WH
    return carry, wrap


def head_masks(rows):
    lane = iota((rows, 128), 1)
    return [(lane // HD) == h for h in range(4)]


NX, NY, NZ = 4, 4, 8
PIECES = (C, 384, 384, 384, 384)
X_FIRST = (True, False, True, False, True)


class Place:
    def __init__(self):
        lon = lax.axis_index("lon")
        lat = lax.axis_index("lat")
        self.lon, self.lat = lon, lat
        self.core = lax.rem(lat, 2)
        self.x = (lon // 32) * 2 + lat // 2
        self.z = lax.rem(lon // 4, 8)
        self.y = lax.rem(lon, 4)

    def at(self, x=None, y=None, z=None, core=None):
        x = self.x if x is None else x
        y = self.y if y is None else y
        z = self.z if z is None else z
        core = self.core if core is None else core
        return ((x // 2) * 32 + z * 4 + y, lax.rem(x, 2) * 2 + core)

    def partner(self):
        return self.at(core=1 - self.core)

    def along(self, axis, step):
        if axis == "core":
            return self.partner()
        if axis == "x":
            return self.at(x=lax.rem(self.x + step, NX))
        if axis == "y":
            return self.at(y=lax.rem(self.y + step, NY))
        return self.at(z=lax.rem(self.z + step, NZ))

    def slab(self, step):
        return (lax.rem(self.lon + 64 + step, 64), self.lat)


def remote(src, dst, send, recv, device):
    return pltpu.make_async_remote_copy(
        src_ref=src, dst_ref=dst, send_sem=send, recv_sem=recv,
        device_id=device, device_id_type=pl.DeviceIdType.MESH,
    )


class Reduction:
    def __init__(self, here, refs, x_first, table):
        self.here = here
        (self.s0, self.r0, self.s1, self.r1, self.s2, self.r2, self.s3, self.r3,
         self.send, self.recv) = refs
        self.axes = ("core", "x", "y", "z") if x_first else ("core", "y", "x", "z")
        self.counts = (2, 4, 4, NZ)
        self.table = table

    def copies(self, stage):
        here = self.here
        axis = self.axes[stage]
        out = []
        for step in range(1, self.counts[stage]):
            target = lax.rem(getattr(here, axis) + step, self.counts[stage])
            if stage == 0:
                src, dst = self.s0.at[target], self.r0
            elif stage == 1:
                src = self.s1.at[target] if axis == "x" else self.s1.at[:, target]
                dst = self.r1.at[step - 1]
            elif stage == 2:
                src, dst = self.s2.at[target], self.r2.at[step - 1]
            else:
                src, dst = self.s3.at[target], self.r3.at[step - 1]
            slot = (0, 1, 4, 7)[stage] + step - 1
            out.append(
                remote(src, dst, self.send.at[slot], self.recv.at[slot], here.along(axis, step))
            )
        return out

    def table_copies(self, stage, arriving):
        if self.table is None:
            return []
        slots, send, recv = (part[stage] for part in self.table)
        axis = self.axes[stage]
        me = getattr(self.here, axis)
        out = []
        for step in range(1, self.counts[stage]):
            n = lax.rem(me + step, self.counts[stage]) if arriving else me
            out.append(
                remote(slots.at[me], slots.at[n], send.at[step], recv.at[n], self.here.along(axis, step))
            )
        return out

    def send_off(self, stage, table_value):
        for copy in self.copies(stage):
            copy.start()
        if self.table is not None:
            self.table[0][stage][getattr(self.here, self.axes[stage])] = table_value
            for copy in self.table_copies(stage, False):
                copy.start()

    def arrived(self, stage):
        for copy in self.copies(stage):
            copy.wait_recv()
        for copy in self.table_copies(stage, True):
            copy.wait_recv()
        if self.table is None:
            return None
        slots = self.table[0][stage]
        total = slots[0]
        for n in range(1, self.counts[stage]):
            total = total + slots[n]
        return total

    def start(self, table_value=None):
        self.send_off(0, table_value)

    def step1(self):
        table_value = self.arrived(0)
        for n in range(NX):
            own = self.s0[self.here.core, n].astype(F32)
            self.s1[n] = (own + self.r0[n].astype(F32)).astype(BF16)
        self.send_off(1, table_value)

    def step2(self):
        table_value = self.arrived(1)
        for n in range(4):
            own = self.s1[self.here.x, n] if self.axes[1] == "x" else self.s1[n, self.here.y]
            total = own.astype(F32)
            for r in range(3):
                total = total + self.r1[r, n].astype(F32)
            self.s2[n] = total.astype(BF16)
        self.send_off(2, table_value)

    def step3(self):
        table_value = self.arrived(2)
        total = self.s2[getattr(self.here, self.axes[2])].astype(F32)
        for r in range(3):
            total = total + self.r2[r].astype(F32)
        for z in range(NZ):
            self.s3[z] = total[2 * z:2 * z + 2]
        self.send_off(3, table_value)

    def step4(self):
        table_value = self.arrived(3)
        total = self.s3[self.here.z]
        for r in range(NZ - 1):
            total = total + self.r3[r]
        return total, table_value

    def finish(self):
        for stage in range(4):
            for copy in self.copies(stage) + self.table_copies(stage, False):
                copy.wait_send()


def body(
    n_dev,
    shift_ref, x_ref, d_ref, wqkv_ref, wproj_ref, gain_ref, table_ref, rel_ref,
    out_ref, gq_ref, gp_ref, gg_ref, gt_ref,
    xw, dw, nx, istd, normed, normed_t, qkv, dh, soft, att_t, dproj, dnorm, dsum, bias, hot, g4, ow, att_p,
    tx_ref, td_ref, back_ref, halo_send, halo_recv, *rest,
):
    here = Place()
    peers = [here.partner(), here.slab(1), here.slab(-1)]
    peers += [here.along("x", n) for n in range(1, NX)]
    peers += [here.along("y", n) for n in range(1, NY)]
    peers += [here.along("z", n) for n in range(1, NZ)]
    barrier = pltpu.get_barrier_semaphore()
    for peer in peers:
        pl.semaphore_signal(barrier, inc=1, device_id=peer, device_id_type=pl.DeviceIdType.MESH)
    pl.semaphore_wait(barrier, len(peers))

    edge = pl.ds(COLS - WW, WW)
    halo = [
        remote(src.at[:, edge, :], dst, halo_send.at[n], halo_recv.at[n], here.slab(1))
        for n, (src, dst) in enumerate(((x_ref, tx_ref), (d_ref, td_ref)))
    ]
    for copy in halo:
        copy.start()

    pieces = []
    for p in range(len(PIECES)):
        refs = rest[p * 10:(p + 1) * 10]
        table = None
        if p:
            base = len(PIECES) * 10 + (p - 1) * 12
            table = (rest[base:base + 4], rest[base + 4:base + 8], rest[base + 8:base + 12])
        pieces.append(Reduction(here, refs, X_FIRST[p], table))

    s = shift_ref[0]
    w_i = iota((128, 128), 0)
    c_i = iota((128, 128), 1)
    to_win = one_hot(c_i == w_i - s)
    t_w = iota((16, 16), 0)
    t_c = iota((16, 16), 1)
    tail_win = one_hot(t_c == t_w - s + 16)
    gain = gain_ref[...]
    grad_scale = (TOK * n_dev) ** (-0.5)

    def shift_row(r, _):
        rows = pl.ds(pl.multiple_of(r * WW, WW), WW)
        for src, dst in ((x_ref, xw), (d_ref, dw)):
            y = mm(to_win, src[r]).astype(BF16)
            for w in range(NWIN):
                dst[w, rows, :] = y[w * WW:(w + 1) * WW]
        return 0

    lax.fori_loop(0, WH, shift_row, 0)

    rel_t = rel_ref[...].astype(F32).T
    code_rows = []
    for wrap in (0, 1):
        for carry in (0, 1):
            j = 112 * wrap + 15 * carry
            row = rel_t[j:j + 1, :]
            code_rows.append(pltpu.roll(jnp.broadcast_to(row, (8, 128)), (128 - j) % 128, 1)[0:1])
    code = jnp.concatenate(code_rows, axis=1).astype(jnp.int32)
    hot[...] = one_hot(iota((512, 512), 0) == code)
    tab = jnp.concatenate([table_ref[...], jnp.zeros((512 - NREL, H), F32)], axis=0).T
    tab = tab * LOG2E
    parts = split3(tab)
    t4 = mm(parts[0], hot[...]) + mm(parts[1], hot[...]) + mm(parts[2], hot[...])
    g4[...] = t4
    carry_m, wrap_m = pair_masks(w_i)
    carry_r, wrap_r = pair_masks(127 - w_i)
    reverse = one_hot(w_i + c_i == 127)

    for h in range(H):
        row = [jnp.broadcast_to(g4[h:h + 1, q * 128:(q + 1) * 128], (128, 128)) for q in range(4)]
        base = jnp.where(
            wrap_m, jnp.where(carry_m, row[3], row[2]), jnp.where(carry_m, row[1], row[0])
        )
        bias[h] = pltpu.roll(base, 0, 1, stride=1, stride_axis=0)

    def norm_win(w, _):
        src = xw[w].astype(F32)
        mean = jnp.mean(src, axis=-1, keepdims=True)
        cen = src - mean
        inv = lax.rsqrt(jnp.mean(cen * cen, axis=-1, keepdims=True) + EPSILON)
        n = cen * inv
        nx[w] = n
        istd[w] = inv
        normed[w] = (n * gain).astype(BF16)
        return 0

    lax.fori_loop(1, NWIN, norm_win, 0)

    row_p = iota((C, C), 0)
    p_core, p_x, p_y = row_p // 256, (row_p // 64) % 4, (row_p // 16) % 4
    p_z, p_t = (row_p // 2) % 8, row_p % 2
    source = (p_x // 2) * 256 + p_z * 32 + p_y * 8 + (p_x % 2) * 4 + p_core * 2 + p_t
    order = one_hot(iota((C, C), 1) == source)

    def project(m, _):
        lhs = normed[pl.ds(2 * m, 2)].reshape(256, C)
        for n in range(3):
            y = mm(lhs, wqkv_ref[:, n * C:(n + 1) * C]).astype(BF16)
            for b in range(4):
                for ww in range(2):
                    qkv[n * 4 + b, 2 * m + ww] = y[ww * 128:(ww + 1) * 128, b * 128:(b + 1) * 128]
        y = mm(dw[pl.ds(2 * m, 2)].reshape(256, C), wproj_ref[...], NT).astype(BF16)
        for b in range(4):
            for ww in range(2):
                dh[b, 2 * m + ww] = y[ww * 128:(ww + 1) * 128, b * 128:(b + 1) * 128]
        normed_t[:, pl.ds(pl.multiple_of(m * 256, 256), 256)] = mm(order, lhs, NT).astype(BF16)
        return 0

    lax.fori_loop(1, 4, project, 0)
    for copy in halo:
        copy.wait_recv()

    def tail_row(r, _):
        rows = pl.ds(pl.multiple_of(r * WW, WW), WW)
        for src, dst in ((tx_ref, xw), (td_ref, dw)):
            y = mm(tail_win, src[r]).astype(BF16)
            dst[0, rows, :] = dst[0, rows, :] + y
        return 0

    lax.fori_loop(0, WH, tail_row, 0)
    norm_win(0, 0)
    project(0, 0)

    masks = head_masks(128)

    def stack_heads(block):
        zero = jnp.zeros_like(block)
        return jnp.concatenate([jnp.where(m, block, zero) for m in masks], axis=0)

    factor2 = HD ** (-0.5) * LOG2E

    def forward(g, w):
        q = qkv[g, w]
        k = qkv[4 + g, w]
        v_t = qkv[8 + g, w].T
        st = mm(k, stack_heads(q), NT)
        cols = pl.ds(pl.multiple_of(w * WIN, WIN), WIN)
        for h in range(4):
            z = st[:, h * 128:(h + 1) * 128] * factor2 + bias[4 * g + h]
            e = jnp.exp2(z - jnp.max(z, axis=0, keepdims=True))
            p = (e * (1.0 / jnp.sum(e, axis=0, keepdims=True))).astype(BF16)
            soft[g, w, :, h * 128:(h + 1) * 128] = p
            a = mm(v_t[h * HD:(h + 1) * HD], p)
            att_t[pl.ds(pl.multiple_of(g * 128 + h * HD, HD), HD), cols] = a.astype(BF16)

    def fwd_step(it, _):
        forward(it // NWIN, it % NWIN)
        return 0

    lax.fori_loop(0, GROUPS * NWIN, fwd_step, 0)

    def order_rows(m, _):
        cols = pl.ds(pl.multiple_of(m * 256, 256), 256)
        att_p[:, cols] = mm(order, att_t[:, cols]).astype(BF16)
        return 0

    lax.fori_loop(0, 4, order_rows, 0)

    def proj_grad(m, _):
        rows = pl.ds(pl.multiple_of(m * 128, 128), 128)
        y = (mm(att_p[rows, :], dw[...].reshape(TOK, C)) * grad_scale).astype(BF16)
        half = m // 2
        for n in range(2):
            for b in range(4):
                k = n * 64 + b * 16
                pieces[0].s0[half, 2 * (m % 2) + n, b] = y[k:k + 16]
        return 0

    lax.fori_loop(0, 4, proj_grad, 0)
    pieces[0].start()

    factor = HD ** (-0.5)

    def backward(g, w):
        q = qkv[g, w]
        k = qkv[4 + g, w]
        v = qkv[8 + g, w]
        dhm = stack_heads(dh[g, w])
        k_t = k.T
        p_all = soft[g, w]
        ds_t = mm(v, dhm, NT)
        low = []
        dq_t = []
        for h in range(4):
            hs = slice(h * 128, (h + 1) * 128)
            p = p_all[:, hs].astype(F32)
            t = p * ds_t[:, hs]
            dsc = t - p * jnp.sum(t, axis=0, keepdims=True)
            dsum[:, hs] = dsum[:, hs] + dsc
            lo = dsc.astype(BF16)
            low.append(lo)
            dq_t.append(mm(k_t[h * HD:(h + 1) * HD], lo))
        dv = mm(p_all, dhm)
        dk = mm(jnp.concatenate(low, axis=1), stack_heads(q)) * factor
        dq = (jnp.concatenate(dq_t, axis=0) * factor).T
        dproj[w, :, 0:128] = dq.astype(BF16)
        dproj[w, :, 128:256] = dk.astype(BF16)
        dproj[w, :, 256:384] = dv.astype(BF16)

    def store(p):
        total, table_sum = pieces[p].step4()
        if p == 0:
            gp_ref[...] = total
        else:
            for b in range(3):
                gq_ref[:, b * C + (p - 1) * 128:b * C + p * 128] = total[:, b * 128:(b + 1) * 128]
            g4[4 * (p - 1):4 * p] = table_sum

    for g in range(GROUPS):
        dsum[...] = jnp.zeros_like(dsum)

        def bwd_step(w, _):
            backward(g, w)
            pl.when(w == 1)(pieces[g].step1)
            pl.when(w == 3)(pieces[g].step2)
            pl.when(w == 5)(pieces[g].step3)
            return 0

        lax.fori_loop(0, NWIN, bwd_step, 0)
        store(g)

        flipped = sum(mm(reverse, part) for part in split3(dsum[...]))
        heads = []
        for h in range(4):
            u = pltpu.roll(flipped[:, h * 128:(h + 1) * 128], 1, 1, stride=1, stride_axis=0)
            cells = []
            for q in range(4):
                keep = (wrap_r if q // 2 else ~wrap_r) & (carry_r if q % 2 else ~carry_r)
                cells.append(jnp.sum(jnp.where(keep, u, 0.0), axis=0, keepdims=True))
            heads.append(jnp.concatenate(cells, axis=1))

        def weight_grad(m, _):
            rows = pl.ds(pl.multiple_of(m * 128, 128), 128)
            y = (mm(normed_t[rows, :], dproj[...].reshape(TOK, 384)) * grad_scale).astype(BF16)
            half = m // 2
            for n in range(2):
                for b in range(4):
                    k = n * 64 + b * 16
                    pieces[g + 1].s0[half, 2 * (m % 2) + n, b] = y[k:k + 16]
            return 0

        lax.fori_loop(0, 4, weight_grad, 0)
        pieces[g + 1].start(jnp.concatenate(heads, axis=0))

        def norm_grad(m, _):
            lhs = dproj[pl.ds(2 * m, 2)].reshape(256, 384)
            w_cols = jnp.concatenate(
                [wqkv_ref[:, b * C + g * 128:b * C + (g + 1) * 128] for b in range(3)], axis=1
            )
            y = mm(lhs, w_cols, NT).reshape(2, WIN, C)
            if g == 0:
                dnorm[pl.ds(2 * m, 2)] = y
            else:
                dnorm[pl.ds(2 * m, 2)] = dnorm[pl.ds(2 * m, 2)] + y
            return 0

        lax.fori_loop(0, 4, norm_grad, 0)

    last = pieces[GROUPS]

    def finish(w, _):
        n = nx[w]
        sc = dnorm[w] * gain
        m1 = jnp.mean(sc, axis=-1, keepdims=True)
        m2 = jnp.mean(sc * n, axis=-1, keepdims=True)
        branch = istd[w] * (sc - m1 - n * m2)
        ow[w] = (dw[w].astype(F32) + branch).astype(BF16)
        return 0

    finish(0, 0)
    home = remote(ow.at[0], back_ref, halo_send.at[2], halo_recv.at[2], here.slab(-1))
    home.start()
    last.step1()
    lax.fori_loop(1, NWIN, finish, 0)
    last.step2()

    to_slab = one_hot(c_i == w_i + s)
    edge_slab = one_hot(t_c == t_w + s - 16)

    def out_row(r, _):
        rows = pl.ds(pl.multiple_of(r * WW, WW), WW)
        src = jnp.concatenate([ow[w, rows, :] for w in range(NWIN)], axis=0)
        out_ref[r] = mm(to_slab, src).astype(BF16)
        return 0

    lax.fori_loop(0, WH, out_row, 0)
    last.step3()

    home.wait_recv()

    def edge_row(r, _):
        rows = pl.ds(pl.multiple_of(r * WW, WW), WW)
        y = mm(edge_slab, back_ref[rows, :]).astype(BF16)
        out_ref[r, COLS - WW:, :] = out_ref[r, COLS - WW:, :] + y
        return 0

    lax.fori_loop(0, WH, edge_row, 0)

    pick = iota((16, C), 1) == 2 * (here.lon * 4 + here.lat) + iota((16, C), 0)
    w_rows = mm(one_hot(pick), wqkv_ref[...])[0:2]
    gain_rows = jnp.sum(jnp.where(pick, jnp.broadcast_to(gain, (16, C)), 0.0), axis=1, keepdims=True)[0:2]

    store(GROUPS)
    gg_ref[...] = jnp.sum(gq_ref[...] * w_rows, axis=1, keepdims=True) / gain_rows

    parts = split3(g4[...])
    total = mm(hot[...], parts[0], NT) + mm(hot[...], parts[1], NT) + mm(hot[...], parts[2], NT)
    gt_ref[...] = total[0:NREL] * ((TOK * n_dev) // WIN) ** (-0.5)

    for piece in pieces:
        piece.finish()
    for copy in halo + [home]:
        copy.wait_send()


def piece_scratch(width):
    return [
        pltpu.VMEM((2, 4, 4, 16, width), BF16),
        pltpu.VMEM((4, 4, 16, width), BF16),
        pltpu.VMEM((4, 4, 16, width), BF16),
        pltpu.VMEM((3, 4, 16, width), BF16),
        pltpu.VMEM((4, 16, width), BF16),
        pltpu.VMEM((3, 16, width), BF16),
        pltpu.VMEM((NZ, 2, width), F32),
        pltpu.VMEM((NZ - 1, 2, width), F32),
        pltpu.SemaphoreType.DMA((14,)),
        pltpu.SemaphoreType.DMA((14,)),
    ]


def table_scratch():
    counts = (2, 4, 4, NZ)
    return (
        [pltpu.VMEM((n, 4, 512), F32) for n in counts]
        + [pltpu.SemaphoreType.DMA((n,)) for n in counts]
        + [pltpu.SemaphoreType.DMA((n,)) for n in counts]
    )


def fused(n_dev, *args):
    vm = pl.BlockSpec(memory_space=pltpu.VMEM)
    return pl.pallas_call(
        functools.partial(body, n_dev),
        out_shape=(
            jax.ShapeDtypeStruct((WH, COLS, C), BF16),
            jax.ShapeDtypeStruct((2, 3 * C), F32),
            jax.ShapeDtypeStruct((2, C), F32),
            jax.ShapeDtypeStruct((2, 1), F32),
            jax.ShapeDtypeStruct((NREL, H), F32),
        ),
        in_specs=[pl.BlockSpec(memory_space=pltpu.SMEM)] + [vm] * 7,
        out_specs=(vm,) * 5,
        scratch_shapes=[
            pltpu.VMEM((NWIN, WIN, C), BF16),
            pltpu.VMEM((NWIN, WIN, C), BF16),
            pltpu.VMEM((NWIN, WIN, C), F32),
            pltpu.VMEM((NWIN, WIN, 1), F32),
            pltpu.VMEM((NWIN, WIN, C), BF16),
            pltpu.VMEM((C, TOK), BF16),
            pltpu.VMEM((12, NWIN, WIN, 128), BF16),
            pltpu.VMEM((GROUPS, NWIN, WIN, 128), BF16),
            pltpu.VMEM((GROUPS, NWIN, WIN, 512), BF16),
            pltpu.VMEM((C, TOK), BF16),
            pltpu.VMEM((NWIN, WIN, 384), BF16),
            pltpu.VMEM((NWIN, WIN, C), F32),
            pltpu.VMEM((WIN, 512), F32),
            pltpu.VMEM((H, WIN, WIN), F32),
            pltpu.VMEM((512, 512), BF16),
            pltpu.VMEM((H, 512), F32),
            pltpu.VMEM((NWIN, WIN, C), BF16),
            pltpu.VMEM((C, TOK), BF16),
            pltpu.VMEM((WH, WW, C), BF16),
            pltpu.VMEM((WH, WW, C), BF16),
            pltpu.VMEM((WIN, C), BF16),
            pltpu.SemaphoreType.DMA((3,)),
            pltpu.SemaphoreType.DMA((3,)),
        ]
        + [ref for width in PIECES for ref in piece_scratch(width)]
        + [ref for _ in range(GROUPS) for ref in table_scratch()],
        compiler_params=pltpu.CompilerParams(
            vmem_limit_bytes=58 * 1024 * 1024, collective_id=0, has_side_effects=True
        ),
        name="fused",
    )(*args)


def shards(inputs, d_out, w_qkv, w_proj, gain, bias_table, rel_index, shifts):
    n_dev = lax.axis_size("lon") * lax.axis_size("lat")
    d_inputs, gq, gp, gg, gt = fused(
        n_dev, shifts, inputs, d_out, w_qkv, w_proj, gain.reshape(1, C), bias_table, rel_index
    )
    return (d_inputs, gq, gp, gg.reshape(2), gt)


def solution(mesh):
    return jax.shard_map(
        shards,
        mesh=mesh,
        in_specs=(P("lat", "lon", None), P("lat", "lon", None), P(), P(), P(), P(), P(), P("lat")),
        out_specs=(
            P("lat", "lon", None),
            P(("lon", "lat"), None),
            P(("lon", "lat"), None),
            P(("lon", "lat")),
            P(),
        ),
        check_vma=False,
    )
```

```python
import functools

import jax
import jax.numpy as jnp
from jax import lax
from jax.experimental import pallas as pl
from jax.experimental.pallas import tpu as pltpu
from jax.sharding import PartitionSpec as P

C = 512
H = 16
HD = 32
WH = 8
WW = 16
WIN = 128
NREL = 465
COLS = 128
NWIN = 8
GROUPS = 4
TOK = NWIN * WIN
EPSILON = 1e-05
LOG2E = 1.4426950408889634
F32 = jnp.float32
BF16 = jnp.bfloat16

NN = (((1,), (0,)), ((), ()))
NT = (((1,), (1,)), ((), ()))


def mm(a, b, dims=NN):
    return lax.dot_general(a, b, dims, preferred_element_type=F32)


def iota(shape, dim):
    return lax.broadcasted_iota(jnp.int32, shape, dim)


def one_hot(cond):
    return jnp.where(cond, 1.0, 0.0).astype(BF16)


def split3(x):
    hi = x.astype(BF16)
    rest = x - hi.astype(F32)
    mid = rest.astype(BF16)
    low = (rest - mid.astype(F32)).astype(BF16)
    return hi, mid, low


def pair_masks(j):
    k = iota((WIN, WIN), 1)
    carry = (j % WW + k % WW) >= WW
    wrap = (j // WW + k // WW + carry.astype(jnp.int32)) >= WH
    return carry, wrap


def head_masks(rows):
    lane = iota((rows, 128), 1)
    return [(lane // HD) == h for h in range(4)]


NX, NY, NZ = 4, 4, 8
PIECES = (C, 384, 384, 384, 384)
TABLE_GROUPS = {3: (0, 1, 2), 4: (3,)}


class Place:
    def __init__(self):
        lon = lax.axis_index("lon")
        lat = lax.axis_index("lat")
        self.lon, self.lat = lon, lat
        self.core = lax.rem(lat, 2)
        self.x = (lon // 32) * 2 + lat // 2
        self.z = lax.rem(lon // 4, 8)
        self.y = lax.rem(lon, 4)
        self.a = self.x + self.core * (self.y - self.x)
        self.b = self.y + self.core * (self.x - self.y)

    def at(self, x=None, y=None, z=None, core=None):
        x = self.x if x is None else x
        y = self.y if y is None else y
        z = self.z if z is None else z
        core = self.core if core is None else core
        return ((x // 2) * 32 + z * 4 + y, lax.rem(x, 2) * 2 + core)

    def partner(self):
        return self.at(core=1 - self.core)

    def along(self, axis, step):
        if axis == "core":
            return self.partner()
        if axis in "ab":
            to_y = self.core if axis == "a" else 1 - self.core
            return self.at(
                x=lax.rem(self.x + (1 - to_y) * step, NX), y=lax.rem(self.y + to_y * step, NY)
            )
        return self.at(z=lax.rem(self.z + step, NZ))

    def slab(self, step):
        return (lax.rem(self.lon + 64 + step, 64), self.lat)


def remote(src, dst, send, recv, device):
    return pltpu.make_async_remote_copy(
        src_ref=src, dst_ref=dst, send_sem=send, recv_sem=recv,
        device_id=device, device_id_type=pl.DeviceIdType.MESH,
    )


class Reduction:
    axes = ("core", "a", "b", "z")
    counts = (2, 4, 4, NZ)

    def __init__(self, here, refs, table):
        self.here = here
        (self.s0, self.r0, self.s1, self.r1, self.s2, self.r2, self.s3, self.r3,
         self.send, self.recv) = refs
        self.table = table

    def copies(self, stage):
        here = self.here
        axis = self.axes[stage]
        out = []
        for step in range(1, self.counts[stage]):
            target = lax.rem(getattr(here, axis) + step, self.counts[stage])
            if stage == 0:
                src, dst = self.s0.at[target], self.r0
            elif stage == 1:
                src, dst = self.s1.at[target], self.r1.at[step - 1]
            elif stage == 2:
                src, dst = self.s2.at[target], self.r2.at[step - 1]
            else:
                src, dst = self.s3.at[target], self.r3.at[step - 1]
            slot = (0, 1, 4, 7)[stage] + step - 1
            out.append(
                remote(src, dst, self.send.at[slot], self.recv.at[slot], here.along(axis, step))
            )
        return out

    def table_copies(self, stage, arriving):
        if self.table is None:
            return []
        slots, send, recv = (part[stage] for part in self.table)
        axis = self.axes[stage]
        me = getattr(self.here, axis)
        out = []
        for step in range(1, self.counts[stage]):
            n = lax.rem(me + step, self.counts[stage]) if arriving else me
            out.append(
                remote(slots.at[me], slots.at[n], send.at[step], recv.at[n], self.here.along(axis, step))
            )
        return out

    def send_off(self, stage, table_value):
        for copy in self.copies(stage):
            copy.start()
        if self.table is not None:
            self.table[0][stage][getattr(self.here, self.axes[stage])] = table_value.astype(BF16)
            for copy in self.table_copies(stage, False):
                copy.start()

    def arrived(self, stage):
        for copy in self.copies(stage):
            copy.wait_recv()
        for copy in self.table_copies(stage, True):
            copy.wait_recv()
        if self.table is None:
            return None
        slots = self.table[0][stage]
        total = slots[0].astype(F32)
        for n in range(1, self.counts[stage]):
            total = total + slots[n].astype(F32)
        return total

    def start(self, table_value=None):
        self.send_off(0, table_value)

    def step1(self):
        table_value = self.arrived(0)
        for n in range(NX):
            own = self.s0[self.here.core, n].astype(F32)
            self.s1[n] = (own + self.r0[n].astype(F32)).astype(BF16)
        self.send_off(1, table_value)

    def step2(self):
        table_value = self.arrived(1)
        for n in range(4):
            total = self.s1[self.here.a, n].astype(F32)
            for r in range(3):
                total = total + self.r1[r, n].astype(F32)
            self.s2[n] = total.astype(BF16)
        self.send_off(2, table_value)

    def step3(self):
        table_value = self.arrived(2)
        total = self.s2[self.here.b].astype(F32)
        for r in range(3):
            total = total + self.r2[r].astype(F32)
        for z in range(NZ):
            self.s3[z] = total[2 * z:2 * z + 2]
        self.send_off(3, table_value)

    def step4(self):
        table_value = self.arrived(3)
        total = self.s3[self.here.z]
        for r in range(NZ - 1):
            total = total + self.r3[r]
        return total, table_value

    def finish(self):
        for stage in range(4):
            for copy in self.copies(stage) + self.table_copies(stage, False):
                copy.wait_send()


def body(
    n_dev,
    shift_ref, x_ref, d_ref, wqkv_ref, wproj_ref, gain_ref, table_ref, rel_ref,
    out_ref, gq_ref, gp_ref, gg_ref, gt_ref,
    xw, dw, nx, istd, normed, normed_t, qkv, dh, soft, att_t, dproj, dnorm, dsum, bias, hot, g4, ow, att_p,
    tx_ref, td_ref, back_ref, halo_send, halo_recv, *rest,
):
    here = Place()
    peers = [here.partner(), here.slab(1), here.slab(-1)]
    peers += [here.along("a", n) for n in range(1, NX)]
    peers += [here.along("b", n) for n in range(1, NY)]
    peers += [here.along("z", n) for n in range(1, NZ)]
    barrier = pltpu.get_barrier_semaphore()
    for peer in peers:
        pl.semaphore_signal(barrier, inc=1, device_id=peer, device_id_type=pl.DeviceIdType.MESH)
    pieces = []
    for p in range(len(PIECES)):
        refs = rest[p * 10:(p + 1) * 10]
        table = None
        if p in TABLE_GROUPS:
            base = len(PIECES) * 10 + 12 * list(TABLE_GROUPS).index(p)
            table = (rest[base:base + 4], rest[base + 4:base + 8], rest[base + 8:base + 12])
        pieces.append(Reduction(here, refs, table))

    s = shift_ref[0]
    w_i = iota((128, 128), 0)
    c_i = iota((128, 128), 1)
    to_win = one_hot(c_i == w_i - s)
    t_w = iota((16, 16), 0)
    t_c = iota((16, 16), 1)
    tail_win = one_hot(t_c == t_w - s + 16)
    gain = gain_ref[...]
    grad_scale = (TOK * n_dev) ** (-0.5)

    def shift_row(r, _):
        rows = pl.ds(pl.multiple_of(r * WW, WW), WW)
        for src, dst in ((x_ref, xw), (d_ref, dw)):
            y = mm(to_win, src[r]).astype(BF16)
            for w in range(NWIN):
                dst[w, rows, :] = y[w * WW:(w + 1) * WW]
        return 0

    lax.fori_loop(0, WH, shift_row, 0)

    pl.semaphore_wait(barrier, len(peers))

    edge = pl.ds(COLS - WW, WW)
    halo = [
        remote(src.at[:, edge, :], dst, halo_send.at[n], halo_recv.at[n], here.slab(1))
        for n, (src, dst) in enumerate(((x_ref, tx_ref), (d_ref, td_ref)))
    ]
    for copy in halo:
        copy.start()

    rel_t = rel_ref[...].astype(F32).T
    code_rows = []
    for wrap in (0, 1):
        for carry in (0, 1):
            j = 112 * wrap + 15 * carry
            row = rel_t[j:j + 1, :]
            code_rows.append(pltpu.roll(jnp.broadcast_to(row, (8, 128)), (128 - j) % 128, 1)[0:1])
    code = jnp.concatenate(code_rows, axis=1).astype(jnp.int32)
    hot[...] = one_hot(iota((512, 512), 0) == code)
    tab = jnp.concatenate([table_ref[...] * LOG2E, jnp.zeros((H, 512 - NREL), F32)], axis=1)
    parts = split3(tab)
    t4 = mm(parts[0], hot[...]) + mm(parts[1], hot[...]) + mm(parts[2], hot[...])
    g4[...] = t4
    carry_m, wrap_m = pair_masks(w_i)
    carry_r, wrap_r = pair_masks(127 - w_i)
    reverse = one_hot(w_i + c_i == 127)

    for h in range(H):
        row = [jnp.broadcast_to(g4[h:h + 1, q * 128:(q + 1) * 128], (128, 128)) for q in range(4)]
        base = jnp.where(
            wrap_m, jnp.where(carry_m, row[3], row[2]), jnp.where(carry_m, row[1], row[0])
        )
        bias[h] = pltpu.roll(base, 0, 1, stride=1, stride_axis=0)

    def norm_win(w, _):
        src = xw[w].astype(F32)
        mean = jnp.mean(src, axis=-1, keepdims=True)
        cen = src - mean
        inv = lax.rsqrt(jnp.mean(cen * cen, axis=-1, keepdims=True) + EPSILON)
        n = cen * inv
        nx[w] = n
        istd[w] = inv
        normed[w] = (n * gain).astype(BF16)
        return 0

    lax.fori_loop(2, NWIN, norm_win, 0)

    row_p = iota((C, C), 0)
    p_core, p_a, p_b = row_p // 256, (row_p // 64) % 4, (row_p // 16) % 4
    p_x = p_a + p_core * (p_b - p_a)
    p_y = p_b + p_core * (p_a - p_b)
    p_z, p_t = (row_p // 2) % 8, row_p % 2
    source = (p_x // 2) * 256 + p_z * 32 + p_y * 8 + (p_x % 2) * 4 + p_core * 2 + p_t
    order = one_hot(iota((C, C), 1) == source)

    def project(m, _):
        lhs = normed[pl.ds(2 * m, 2)].reshape(256, C)
        for n in range(3):
            y = mm(lhs, wqkv_ref[:, n * C:(n + 1) * C]).astype(BF16)
            for b in range(4):
                for ww in range(2):
                    qkv[n * 4 + b, 2 * m + ww] = y[ww * 128:(ww + 1) * 128, b * 128:(b + 1) * 128]
        y = mm(dw[pl.ds(2 * m, 2)].reshape(256, C), wproj_ref[...], NT).astype(BF16)
        for b in range(4):
            for ww in range(2):
                dh[b, 2 * m + ww] = y[ww * 128:(ww + 1) * 128, b * 128:(b + 1) * 128]
        normed_t[:, pl.ds(pl.multiple_of(m * 256, 256), 256)] = mm(order, lhs, NT).astype(BF16)
        return 0

    lax.fori_loop(1, 4, project, 0)
    masks = head_masks(128)

    def stack_heads(block):
        zero = jnp.zeros_like(block)
        return jnp.concatenate([jnp.where(m, block, zero) for m in masks], axis=0)

    factor2 = HD ** (-0.5) * LOG2E

    def forward(g, w):
        q = qkv[g, w]
        k = qkv[4 + g, w]
        v_t = qkv[8 + g, w].T
        st = mm(k, stack_heads(q), NT)
        cols = pl.ds(pl.multiple_of(w * WIN, WIN), WIN)
        for h in range(4):
            z = st[:, h * 128:(h + 1) * 128] * factor2 + bias[4 * g + h]
            e = jnp.exp2(z - jnp.max(z, axis=0, keepdims=True))
            p = (e * (1.0 / jnp.sum(e, axis=0, keepdims=True))).astype(BF16)
            soft[g, w, :, h * 128:(h + 1) * 128] = p
            a = mm(v_t[h * HD:(h + 1) * HD], p)
            att_t[pl.ds(pl.multiple_of(g * 128 + h * HD, HD), HD), cols] = a.astype(BF16)

    def fwd_step(it, _):
        forward(it // (NWIN - 2), 2 + it % (NWIN - 2))
        return 0

    lax.fori_loop(0, GROUPS * (NWIN - 2), fwd_step, 0)

    for copy in halo:
        copy.wait_recv()

    def tail_row(r, _):
        rows = pl.ds(pl.multiple_of(r * WW, WW), WW)
        for src, dst in ((tx_ref, xw), (td_ref, dw)):
            y = mm(tail_win, src[r]).astype(BF16)
            dst[0, rows, :] = dst[0, rows, :] + y
        return 0

    lax.fori_loop(0, WH, tail_row, 0)
    lax.fori_loop(0, 2, norm_win, 0)
    project(0, 0)

    def fwd_late(it, _):
        forward(it // 2, it % 2)
        return 0

    lax.fori_loop(0, GROUPS * 2, fwd_late, 0)

    def order_rows(m, _):
        cols = pl.ds(pl.multiple_of(m * 256, 256), 256)
        att_p[:, cols] = mm(order, att_t[:, cols]).astype(BF16)
        return 0

    lax.fori_loop(0, 4, order_rows, 0)

    def proj_grad(m, _):
        rows = pl.ds(pl.multiple_of(m * 128, 128), 128)
        y = (mm(att_p[rows, :], dw[...].reshape(TOK, C)) * grad_scale).astype(BF16)
        half = m // 2
        for n in range(2):
            for b in range(4):
                k = n * 64 + b * 16
                pieces[0].s0[half, 2 * (m % 2) + n, b] = y[k:k + 16]
        return 0

    lax.fori_loop(0, 4, proj_grad, 0)
    pieces[0].start()

    factor = HD ** (-0.5)

    def backward(g, w):
        q = qkv[g, w]
        k = qkv[4 + g, w]
        v = qkv[8 + g, w]
        dhm = stack_heads(dh[g, w])
        k_t = k.T
        p_all = soft[g, w]
        ds_t = mm(v, dhm, NT)
        low = []
        dq_t = []
        for h in range(4):
            hs = slice(h * 128, (h + 1) * 128)
            p = p_all[:, hs].astype(F32)
            t = p * ds_t[:, hs]
            dsc = t - p * jnp.sum(t, axis=0, keepdims=True)
            dsum[:, hs] = dsum[:, hs] + dsc
            lo = dsc.astype(BF16)
            low.append(lo)
            dq_t.append(mm(k_t[h * HD:(h + 1) * HD], lo))
        dv = mm(p_all, dhm)
        dk = mm(jnp.concatenate(low, axis=1), stack_heads(q)) * factor
        dq = (jnp.concatenate(dq_t, axis=0) * factor).T
        dproj[0, g, w] = dq.astype(BF16)
        dproj[1, g, w] = dk.astype(BF16)
        dproj[2, g, w] = dv.astype(BF16)

    def store(p):
        total, table_sum = pieces[p].step4()
        if p == 0:
            gp_ref[...] = total
        else:
            for b in range(3):
                gq_ref[:, b * C + (p - 1) * 128:b * C + p * 128] = total[:, b * 128:(b + 1) * 128]
        if p in TABLE_GROUPS:
            for n, group in enumerate(TABLE_GROUPS[p]):
                for h in range(4):
                    for q in range(4):
                        r = 16 * n + 4 * h + q
                        g4[4 * group + h:4 * group + h + 1, q * 128:(q + 1) * 128] = table_sum[r:r + 1]

    bias_sums = {}
    for g in range(GROUPS):
        dsum[...] = jnp.zeros_like(dsum)

        def bwd_step(w, _):
            backward(g, w)
            if g:
                pl.when(w == 1)(pieces[g - 1].step3)
                pl.when(w == 5)(functools.partial(store, g - 1))
            pl.when(w == 2)(pieces[g].step1)
            pl.when(w == 7)(pieces[g].step2)
            return 0

        lax.fori_loop(0, NWIN, bwd_step, 0)

        flipped = sum(mm(reverse, part) for part in split3(dsum[...]))
        heads = bias_sums.setdefault(min(p for p in TABLE_GROUPS if g in TABLE_GROUPS[p]), [])
        for h in range(4):
            u = pltpu.roll(flipped[:, h * 128:(h + 1) * 128], 1, 1, stride=1, stride_axis=0)
            for q in range(4):
                keep = (wrap_r if q // 2 else ~wrap_r) & (carry_r if q % 2 else ~carry_r)
                heads.append(jnp.sum(jnp.where(keep, u, 0.0), axis=0, keepdims=True))

        def weight_grad(m, _):
            rows = pl.ds(pl.multiple_of(m * 128, 128), 128)
            y = jnp.concatenate(
                [mm(normed_t[rows, :], dproj[b, g].reshape(TOK, 128)) for b in range(3)], axis=1
            )
            y = (y * grad_scale).astype(BF16)
            half = m // 2
            for n in range(2):
                for b in range(4):
                    k = n * 64 + b * 16
                    pieces[g + 1].s0[half, 2 * (m % 2) + n, b] = y[k:k + 16]
            return 0

        lax.fori_loop(0, 4, weight_grad, 0)
        pieces[g + 1].start(
            jnp.concatenate(bias_sums[g + 1], axis=0) if g + 1 in TABLE_GROUPS else None
        )

    def norm_grad(m, _):
        lhs = jnp.concatenate(
            [dproj[b, g, pl.ds(2 * m, 2)].reshape(256, 128) for b in range(3) for g in range(GROUPS)],
            axis=1,
        )
        dnorm[pl.ds(2 * m, 2)] = mm(lhs, wqkv_ref[...], NT).reshape(2, WIN, C)
        return 0

    last = pieces[GROUPS]

    def finish(w, _):
        n = nx[w]
        sc = dnorm[w] * gain
        m1 = jnp.mean(sc, axis=-1, keepdims=True)
        m2 = jnp.mean(sc * n, axis=-1, keepdims=True)
        branch = istd[w] * (sc - m1 - n * m2)
        ow[w] = (dw[w].astype(F32) + branch).astype(BF16)
        return 0

    norm_grad(0, 0)
    finish(0, 0)
    home = remote(ow.at[0], back_ref, halo_send.at[2], halo_recv.at[2], here.slab(-1))
    home.start()
    pieces[GROUPS - 1].step3()
    last.step1()
    lax.fori_loop(1, 4, norm_grad, 0)
    store(GROUPS - 1)
    last.step2()
    lax.fori_loop(1, NWIN, finish, 0)

    to_slab = one_hot(c_i == w_i + s)
    edge_slab = one_hot(t_c == t_w + s - 16)

    def out_row(r, _):
        rows = pl.ds(pl.multiple_of(r * WW, WW), WW)
        src = jnp.concatenate([ow[w, rows, :] for w in range(NWIN)], axis=0)
        out_ref[r] = mm(to_slab, src).astype(BF16)
        return 0

    last.step3()
    lax.fori_loop(0, WH, out_row, 0)

    home.wait_recv()

    def edge_row(r, _):
        rows = pl.ds(pl.multiple_of(r * WW, WW), WW)
        y = mm(edge_slab, back_ref[rows, :]).astype(BF16)
        out_ref[r, COLS - WW:, :] = out_ref[r, COLS - WW:, :] + y
        return 0

    lax.fori_loop(0, WH, edge_row, 0)

    pick = iota((16, C), 1) == 2 * (here.lon * 4 + here.lat) + iota((16, C), 0)
    w_rows = mm(one_hot(pick), wqkv_ref[...])[0:2]
    gain_rows = jnp.sum(jnp.where(pick, jnp.broadcast_to(gain, (16, C)), 0.0), axis=1, keepdims=True)[0:2]

    store(GROUPS)
    gg = jnp.sum(gq_ref[...] * w_rows, axis=1, keepdims=True) / gain_rows
    gg_ref[...] = jnp.where(iota((1, 2), 1) == 0, gg[0:1], gg[1:2])

    parts = split3(g4[...])
    total = mm(parts[0], hot[...], NT) + mm(parts[1], hot[...], NT) + mm(parts[2], hot[...], NT)
    gt_ref[...] = total[:, 0:NREL] * ((TOK * n_dev) // WIN) ** (-0.5)

    for piece in pieces:
        piece.finish()
    for copy in halo + [home]:
        copy.wait_send()


def piece_scratch(width):
    return [
        pltpu.VMEM((2, 4, 4, 16, width), BF16),
        pltpu.VMEM((4, 4, 16, width), BF16),
        pltpu.VMEM((4, 4, 16, width), BF16),
        pltpu.VMEM((3, 4, 16, width), BF16),
        pltpu.VMEM((4, 16, width), BF16),
        pltpu.VMEM((3, 16, width), BF16),
        pltpu.VMEM((NZ, 2, width), F32),
        pltpu.VMEM((NZ - 1, 2, width), F32),
        pltpu.SemaphoreType.DMA((14,)),
        pltpu.SemaphoreType.DMA((14,)),
    ]


def table_scratch(groups):
    counts = Reduction.counts
    return (
        [pltpu.VMEM((n, 16 * groups, 128), BF16) for n in counts]
        + [pltpu.SemaphoreType.DMA((n,)) for n in counts]
        + [pltpu.SemaphoreType.DMA((n,)) for n in counts]
    )


def fused(n_dev, *args):
    vm = pl.BlockSpec(memory_space=pltpu.VMEM)
    return pl.pallas_call(
        functools.partial(body, n_dev),
        out_shape=(
            jax.ShapeDtypeStruct((WH, COLS, C), BF16),
            jax.ShapeDtypeStruct((2, 3 * C), F32),
            jax.ShapeDtypeStruct((2, C), F32),
            jax.ShapeDtypeStruct((1, 2), F32),
            jax.ShapeDtypeStruct((H, NREL), F32),
        ),
        in_specs=[pl.BlockSpec(memory_space=pltpu.SMEM)] + [vm] * 7,
        out_specs=(vm,) * 5,
        scratch_shapes=[
            pltpu.VMEM((NWIN, WIN, C), BF16),
            pltpu.VMEM((NWIN, WIN, C), BF16),
            pltpu.VMEM((NWIN, WIN, C), F32),
            pltpu.VMEM((NWIN, WIN, 1), F32),
            pltpu.VMEM((NWIN, WIN, C), BF16),
            pltpu.VMEM((C, TOK), BF16),
            pltpu.VMEM((12, NWIN, WIN, 128), BF16),
            pltpu.VMEM((GROUPS, NWIN, WIN, 128), BF16),
            pltpu.VMEM((GROUPS, NWIN, WIN, 512), BF16),
            pltpu.VMEM((C, TOK), BF16),
            pltpu.VMEM((3, GROUPS, NWIN, WIN, 128), BF16),
            pltpu.VMEM((NWIN, WIN, C), F32),
            pltpu.VMEM((WIN, 512), F32),
            pltpu.VMEM((H, WIN, WIN), F32),
            pltpu.VMEM((512, 512), BF16),
            pltpu.VMEM((H, 512), F32),
            pltpu.VMEM((NWIN, WIN, C), BF16),
            pltpu.VMEM((C, TOK), BF16),
            pltpu.VMEM((WH, WW, C), BF16),
            pltpu.VMEM((WH, WW, C), BF16),
            pltpu.VMEM((WIN, C), BF16),
            pltpu.SemaphoreType.DMA((3,)),
            pltpu.SemaphoreType.DMA((3,)),
        ]
        + [ref for width in PIECES for ref in piece_scratch(width)]
        + [ref for groups in TABLE_GROUPS.values() for ref in table_scratch(len(groups))],
        compiler_params=pltpu.CompilerParams(
            vmem_limit_bytes=58 * 1024 * 1024, collective_id=0, has_side_effects=True
        ),
        name="fused",
    )(*args)


def shards(inputs, d_out, w_qkv, w_proj, gain, bias_table, rel_index, shifts):
    n_dev = lax.axis_size("lon") * lax.axis_size("lat")
    d_inputs, gq, gp, gg, gt = fused(
        n_dev, shifts, inputs, d_out, w_qkv, w_proj, gain.reshape(1, C), bias_table.T, rel_index
    )
    return (d_inputs, gq, gp, gg.reshape(2), gt.T)


def solution(mesh):
    return jax.shard_map(
        shards,
        mesh=mesh,
        in_specs=(P("lat", "lon", None), P("lat", "lon", None), P(), P(), P(), P(), P(), P("lat")),
        out_specs=(
            P("lat", "lon", None),
            P(("lon", "lat"), None),
            P(("lon", "lat"), None),
            P(("lon", "lat")),
            P(),
        ),
        check_vma=False,
    )
```

```python
import functools

import jax
import jax.numpy as jnp
from jax import lax
from jax.experimental import pallas as pl
from jax.experimental.pallas import tpu as pltpu
from jax.sharding import PartitionSpec as P

C = 512
H = 16
HD = 32
WH = 8
WW = 16
WIN = 128
NREL = 465
COLS = 128
NWIN = 8
GROUPS = 4
TOK = NWIN * WIN
EPSILON = 1e-05
LOG2E = 1.4426950408889634
F32 = jnp.float32
BF16 = jnp.bfloat16

NN = (((1,), (0,)), ((), ()))
NT = (((1,), (1,)), ((), ()))


def mm(a, b, dims=NN):
    return lax.dot_general(a, b, dims, preferred_element_type=F32)


def iota(shape, dim):
    return lax.broadcasted_iota(jnp.int32, shape, dim)


def one_hot(cond):
    return jnp.where(cond, 1.0, 0.0).astype(BF16)


def split3(x):
    hi = x.astype(BF16)
    rest = x - hi.astype(F32)
    mid = rest.astype(BF16)
    low = (rest - mid.astype(F32)).astype(BF16)
    return hi, mid, low


def pair_masks(j):
    k = iota((WIN, WIN), 1)
    carry = (j % WW + k % WW) >= WW
    wrap = (j // WW + k // WW + carry.astype(jnp.int32)) >= WH
    return carry, wrap


def head_masks(rows):
    lane = iota((rows, 128), 1)
    return [(lane // HD) == h for h in range(4)]


NX, NY, NZ = 4, 4, 8
PIECES = (C, 384, 384, 384, 384)
TABLE_GROUPS = {3: (0, 1, 2), 4: (3,)}


class Place:
    def __init__(self):
        lon = lax.axis_index("lon")
        lat = lax.axis_index("lat")
        self.lon, self.lat = lon, lat
        self.core = lax.rem(lat, 2)
        self.x = (lon // 32) * 2 + lat // 2
        self.z = lax.rem(lon // 4, 8)
        self.y = lax.rem(lon, 4)
        self.a = self.x + self.core * (self.y - self.x)
        self.b = self.y + self.core * (self.x - self.y)

    def at(self, x=None, y=None, z=None, core=None):
        x = self.x if x is None else x
        y = self.y if y is None else y
        z = self.z if z is None else z
        core = self.core if core is None else core
        return ((x // 2) * 32 + z * 4 + y, lax.rem(x, 2) * 2 + core)

    def partner(self):
        return self.at(core=1 - self.core)

    def along(self, axis, step):
        if axis == "core":
            return self.partner()
        if axis in "ab":
            to_y = self.core if axis == "a" else 1 - self.core
            return self.at(
                x=lax.rem(self.x + (1 - to_y) * step, NX), y=lax.rem(self.y + to_y * step, NY)
            )
        return self.at(z=lax.rem(self.z + step, NZ))

    def slab(self, step):
        return (lax.rem(self.lon + 64 + step, 64), self.lat)


def remote(src, dst, send, recv, device):
    return pltpu.make_async_remote_copy(
        src_ref=src, dst_ref=dst, send_sem=send, recv_sem=recv,
        device_id=device, device_id_type=pl.DeviceIdType.MESH,
    )


class Reduction:
    axes = ("core", "a", "b", "z")
    counts = (2, 4, 4, NZ)

    def __init__(self, here, refs, table):
        self.here = here
        (self.s0, self.r0, self.s1, self.r1, self.s2, self.r2, self.s3, self.r3,
         self.send, self.recv) = refs
        self.table = table

    def copies(self, stage):
        here = self.here
        axis = self.axes[stage]
        out = []
        for step in range(1, self.counts[stage]):
            target = lax.rem(getattr(here, axis) + step, self.counts[stage])
            if stage == 0:
                src, dst = self.s0.at[target], self.r0
            elif stage == 1:
                src, dst = self.s1.at[target], self.r1.at[step - 1]
            elif stage == 2:
                src, dst = self.s2.at[target], self.r2.at[step - 1]
            else:
                src, dst = self.s3.at[target], self.r3.at[step - 1]
            slot = (0, 1, 4, 7)[stage] + step - 1
            out.append(
                remote(src, dst, self.send.at[slot], self.recv.at[slot], here.along(axis, step))
            )
        return out

    def table_copies(self, stage, arriving):
        if self.table is None:
            return []
        slots, send, recv = (part[stage] for part in self.table)
        axis = self.axes[stage]
        me = getattr(self.here, axis)
        out = []
        for step in range(1, self.counts[stage]):
            n = lax.rem(me + step, self.counts[stage]) if arriving else me
            out.append(
                remote(slots.at[me], slots.at[n], send.at[step], recv.at[n], self.here.along(axis, step))
            )
        return out

    def send_off(self, stage, table_value):
        for copy in self.copies(stage):
            copy.start()
        if self.table is not None:
            self.table[0][stage][getattr(self.here, self.axes[stage])] = table_value.astype(BF16)
            for copy in self.table_copies(stage, False):
                copy.start()

    def arrived(self, stage):
        for copy in self.copies(stage):
            copy.wait_recv()
        for copy in self.table_copies(stage, True):
            copy.wait_recv()
        if self.table is None:
            return None
        slots = self.table[0][stage]
        total = slots[0].astype(F32)
        for n in range(1, self.counts[stage]):
            total = total + slots[n].astype(F32)
        return total

    def start(self, table_value=None):
        self.send_off(0, table_value)

    def step1(self):
        table_value = self.arrived(0)
        for n in range(NX):
            own = self.s0[self.here.core, n].astype(F32)
            self.s1[n] = (own + self.r0[n].astype(F32)).astype(BF16)
        self.send_off(1, table_value)

    def step2(self):
        table_value = self.arrived(1)
        for n in range(4):
            total = self.s1[self.here.a, n].astype(F32)
            for r in range(3):
                total = total + self.r1[r, n].astype(F32)
            self.s2[n] = total.astype(BF16)
        self.send_off(2, table_value)

    def step3(self):
        table_value = self.arrived(2)
        total = self.s2[self.here.b].astype(F32)
        for r in range(3):
            total = total + self.r2[r].astype(F32)
        for z in range(NZ):
            self.s3[z] = total[2 * z:2 * z + 2]
        self.send_off(3, table_value)

    def step4(self):
        table_value = self.arrived(3)
        total = self.s3[self.here.z]
        for r in range(NZ - 1):
            total = total + self.r3[r]
        return total, table_value

    def finish(self):
        for stage in range(4):
            for copy in self.copies(stage) + self.table_copies(stage, False):
                copy.wait_send()


def body(
    n_dev,
    shift_ref, x_ref, d_ref, wqkv_ref, wproj_ref, gain_ref, table_ref, rel_ref,
    out_ref, gq_ref, gp_ref, gg_ref, gt_ref,
    xw, dw, nx, istd, normed, normed_t, qkv, dh, soft, att_t, dproj, dnorm, dsum, bias, hot, g4, ow, att_p,
    tx_ref, td_ref, back_ref, halo_send, halo_recv, *rest,
):
    here = Place()
    peers = [here.partner(), here.slab(1), here.slab(-1)]
    peers += [here.along("a", n) for n in range(1, NX)]
    peers += [here.along("b", n) for n in range(1, NY)]
    peers += [here.along("z", n) for n in range(1, NZ)]
    barrier = pltpu.get_barrier_semaphore()
    for peer in peers:
        pl.semaphore_signal(barrier, inc=1, device_id=peer, device_id_type=pl.DeviceIdType.MESH)
    pieces = []
    for p in range(len(PIECES)):
        refs = rest[p * 10:(p + 1) * 10]
        table = None
        if p in TABLE_GROUPS:
            base = len(PIECES) * 10 + 12 * list(TABLE_GROUPS).index(p)
            table = (rest[base:base + 4], rest[base + 4:base + 8], rest[base + 8:base + 12])
        pieces.append(Reduction(here, refs, table))

    s = shift_ref[0]
    w_i = iota((128, 128), 0)
    c_i = iota((128, 128), 1)
    to_win = one_hot(c_i == w_i - s)
    t_w = iota((16, 16), 0)
    t_c = iota((16, 16), 1)
    tail_win = one_hot(t_c == t_w - s + 16)
    gain = gain_ref[...]
    grad_scale = (TOK * n_dev) ** (-0.5)

    def shift_row(r, _):
        rows = pl.ds(pl.multiple_of(r * WW, WW), WW)
        for src, dst in ((x_ref, xw), (d_ref, dw)):
            y = mm(to_win, src[r]).astype(BF16)
            for w in range(NWIN):
                dst[w, rows, :] = y[w * WW:(w + 1) * WW]
        return 0

    lax.fori_loop(0, WH, shift_row, 0)

    pl.semaphore_wait(barrier, len(peers))

    edge = pl.ds(COLS - WW, WW)
    halo = [
        remote(src.at[:, edge, :], dst, halo_send.at[n], halo_recv.at[n], here.slab(1))
        for n, (src, dst) in enumerate(((x_ref, tx_ref), (d_ref, td_ref)))
    ]
    for copy in halo:
        copy.start()

    rel_t = rel_ref[...].astype(F32).T
    code_rows = []
    for wrap in (0, 1):
        for carry in (0, 1):
            j = 112 * wrap + 15 * carry
            row = rel_t[j:j + 1, :]
            code_rows.append(pltpu.roll(jnp.broadcast_to(row, (8, 128)), (128 - j) % 128, 1)[0:1])
    code = jnp.concatenate(code_rows, axis=1).astype(jnp.int32)
    hot[...] = one_hot(iota((512, 512), 0) == code)
    tab = jnp.concatenate([table_ref[...] * LOG2E, jnp.zeros((H, 512 - NREL), F32)], axis=1)
    parts = split3(tab)
    t4 = mm(parts[0], hot[...]) + mm(parts[1], hot[...]) + mm(parts[2], hot[...])
    g4[...] = t4
    carry_m, wrap_m = pair_masks(w_i)
    carry_r, wrap_r = pair_masks(127 - w_i)
    reverse = one_hot(w_i + c_i == 127)

    for h in range(H):
        row = [jnp.broadcast_to(g4[h:h + 1, q * 128:(q + 1) * 128], (128, 128)) for q in range(4)]
        base = jnp.where(
            wrap_m, jnp.where(carry_m, row[3], row[2]), jnp.where(carry_m, row[1], row[0])
        )
        bias[h] = pltpu.roll(base, 0, 1, stride=1, stride_axis=0)

    def norm_win(w, _):
        src = xw[w].astype(F32)
        mean = jnp.mean(src, axis=-1, keepdims=True)
        cen = src - mean
        inv = lax.rsqrt(jnp.mean(cen * cen, axis=-1, keepdims=True) + EPSILON)
        n = cen * inv
        nx[w] = n
        istd[w] = inv
        normed[w] = (n * gain).astype(BF16)
        return 0

    lax.fori_loop(2, NWIN, norm_win, 0)

    row_p = iota((C, C), 0)
    p_core, p_a, p_b = row_p // 256, (row_p // 64) % 4, (row_p // 16) % 4
    p_x = p_a + p_core * (p_b - p_a)
    p_y = p_b + p_core * (p_a - p_b)
    p_z, p_t = (row_p // 2) % 8, row_p % 2
    source = (p_x // 2) * 256 + p_z * 32 + p_y * 8 + (p_x % 2) * 4 + p_core * 2 + p_t
    order = one_hot(iota((C, C), 1) == source)

    def project(m, _):
        lhs = normed[pl.ds(2 * m, 2)].reshape(256, C)
        for n in range(3):
            y = mm(lhs, wqkv_ref[:, n * C:(n + 1) * C]).astype(BF16)
            for b in range(4):
                for ww in range(2):
                    qkv[n * 4 + b, 2 * m + ww] = y[ww * 128:(ww + 1) * 128, b * 128:(b + 1) * 128]
        y = mm(dw[pl.ds(2 * m, 2)].reshape(256, C), wproj_ref[...], NT).astype(BF16)
        for b in range(4):
            for ww in range(2):
                dh[b, 2 * m + ww] = y[ww * 128:(ww + 1) * 128, b * 128:(b + 1) * 128]
        normed_t[:, pl.ds(pl.multiple_of(m * 256, 256), 256)] = mm(order, lhs, NT).astype(BF16)
        return 0

    lax.fori_loop(1, 4, project, 0)
    masks = head_masks(128)

    def stack_heads(block):
        zero = jnp.zeros_like(block)
        return jnp.concatenate([jnp.where(m, block, zero) for m in masks], axis=0)

    factor2 = HD ** (-0.5) * LOG2E

    def forward(g, w):
        q = qkv[g, w]
        k = qkv[4 + g, w]
        v_t = qkv[8 + g, w].T
        st = mm(k, stack_heads(q), NT)
        cols = pl.ds(pl.multiple_of(w * WIN, WIN), WIN)
        for h in range(4):
            z = st[:, h * 128:(h + 1) * 128] * factor2 + bias[4 * g + h]
            e = jnp.exp2(z - jnp.max(z, axis=0, keepdims=True))
            p = (e * (1.0 / jnp.sum(e, axis=0, keepdims=True))).astype(BF16)
            soft[g, w, :, h * 128:(h + 1) * 128] = p
            a = mm(v_t[h * HD:(h + 1) * HD], p)
            att_t[pl.ds(pl.multiple_of(g * 128 + h * HD, HD), HD), cols] = a.astype(BF16)

    def fwd_step(it, _):
        forward(it // 3, 2 + 2 * (it % 3))
        forward(it // 3, 3 + 2 * (it % 3))
        return 0

    lax.fori_loop(0, GROUPS * 3, fwd_step, 0)

    for copy in halo:
        copy.wait_recv()

    def tail_row(r, _):
        rows = pl.ds(pl.multiple_of(r * WW, WW), WW)
        for src, dst in ((tx_ref, xw), (td_ref, dw)):
            y = mm(tail_win, src[r]).astype(BF16)
            dst[0, rows, :] = dst[0, rows, :] + y
        return 0

    lax.fori_loop(0, WH, tail_row, 0)
    lax.fori_loop(0, 2, norm_win, 0)
    project(0, 0)

    def fwd_late(g, _):
        forward(g, 0)
        forward(g, 1)
        return 0

    lax.fori_loop(0, GROUPS, fwd_late, 0)

    def order_rows(m, _):
        cols = pl.ds(pl.multiple_of(m * 256, 256), 256)
        att_p[:, cols] = mm(order, att_t[:, cols]).astype(BF16)
        return 0

    lax.fori_loop(0, 4, order_rows, 0)

    def to_send(piece, y):
        y = (y * grad_scale).astype(BF16)
        for n in range(32):
            piece.s0[n // 16, (n // 4) % 4, n % 4] = y[n * 16:(n + 1) * 16]

    to_send(pieces[0], mm(att_p[...], dw[...].reshape(TOK, C)))
    pieces[0].start()

    factor = HD ** (-0.5)

    def backward(g, w):
        q = qkv[g, w]
        k = qkv[4 + g, w]
        v = qkv[8 + g, w]
        dhm = stack_heads(dh[g, w])
        k_t = k.T
        p_all = soft[g, w]
        ds_t = mm(v, dhm, NT)
        low = []
        dq_t = []
        for h in range(4):
            hs = slice(h * 128, (h + 1) * 128)
            p = p_all[:, hs].astype(F32)
            t = p * ds_t[:, hs]
            dsc = t - p * jnp.sum(t, axis=0, keepdims=True)
            dsum[:, hs] = dsum[:, hs] + dsc
            lo = dsc.astype(BF16)
            low.append(lo)
            dq_t.append(mm(k_t[h * HD:(h + 1) * HD], lo))
        dv = mm(p_all, dhm)
        dk = mm(jnp.concatenate(low, axis=1), stack_heads(q)) * factor
        dq = (jnp.concatenate(dq_t, axis=0) * factor).T
        dproj[0, g, w] = dq.astype(BF16)
        dproj[1, g, w] = dk.astype(BF16)
        dproj[2, g, w] = dv.astype(BF16)

    def store(p):
        total, table_sum = pieces[p].step4()
        if p == 0:
            gp_ref[...] = total
        else:
            for b in range(3):
                gq_ref[:, b * C + (p - 1) * 128:b * C + p * 128] = total[:, b * 128:(b + 1) * 128]
        if p in TABLE_GROUPS:
            for n, group in enumerate(TABLE_GROUPS[p]):
                for h in range(4):
                    for q in range(4):
                        r = 16 * n + 4 * h + q
                        g4[4 * group + h:4 * group + h + 1, q * 128:(q + 1) * 128] = table_sum[r:r + 1]

    bias_sums = {}
    for g in range(GROUPS):
        dsum[...] = jnp.zeros_like(dsum)

        def bwd_step(i, _):
            backward(g, 2 * i)
            backward(g, 2 * i + 1)
            if g >= 1:
                pl.when(i == 0)(pieces[g - 1].step2)
            if g >= 2:
                pl.when(i == 0)(pieces[g - 2].step3)
                pl.when(i == 3)(functools.partial(store, g - 2))
            pl.when(i == 1)(pieces[g].step1)
            return 0

        lax.fori_loop(0, NWIN // 2, bwd_step, 0)

        flipped = sum(mm(reverse, part) for part in split3(dsum[...]))
        heads = bias_sums.setdefault(min(p for p in TABLE_GROUPS if g in TABLE_GROUPS[p]), [])
        for h in range(4):
            u = pltpu.roll(flipped[:, h * 128:(h + 1) * 128], 1, 1, stride=1, stride_axis=0)
            for q in range(4):
                keep = (wrap_r if q // 2 else ~wrap_r) & (carry_r if q % 2 else ~carry_r)
                heads.append(jnp.sum(jnp.where(keep, u, 0.0), axis=0, keepdims=True))

        grads = jnp.concatenate([dproj[b, g].reshape(TOK, 128) for b in range(3)], axis=1)
        to_send(pieces[g + 1], mm(normed_t[...], grads))
        pieces[g + 1].start(
            jnp.concatenate(bias_sums[g + 1], axis=0) if g + 1 in TABLE_GROUPS else None
        )

    def norm_grad(m, _):
        lhs = jnp.concatenate(
            [dproj[b, g, pl.ds(2 * m, 2)].reshape(256, 128) for b in range(3) for g in range(GROUPS)],
            axis=1,
        )
        dnorm[pl.ds(2 * m, 2)] = mm(lhs, wqkv_ref[...], NT).reshape(2, WIN, C)
        return 0

    last = pieces[GROUPS]

    def finish(w, _):
        n = nx[w]
        sc = dnorm[w] * gain
        m1 = jnp.mean(sc, axis=-1, keepdims=True)
        m2 = jnp.mean(sc * n, axis=-1, keepdims=True)
        branch = istd[w] * (sc - m1 - n * m2)
        ow[w] = (dw[w].astype(F32) + branch).astype(BF16)
        return 0

    norm_grad(0, 0)
    finish(0, 0)
    home = remote(ow.at[0], back_ref, halo_send.at[2], halo_recv.at[2], here.slab(-1))
    home.start()
    pieces[GROUPS - 2].step3()
    pieces[GROUPS - 1].step2()
    last.step1()
    norm_grad(1, 0)
    norm_grad(2, 0)
    pieces[GROUPS - 1].step3()
    norm_grad(3, 0)
    store(GROUPS - 2)
    last.step2()
    lax.fori_loop(1, NWIN, finish, 0)

    to_slab = one_hot(c_i == w_i + s)
    edge_slab = one_hot(t_c == t_w + s - 16)

    def out_row(r, _):
        rows = pl.ds(pl.multiple_of(r * WW, WW), WW)
        src = jnp.concatenate([ow[w, rows, :] for w in range(NWIN)], axis=0)
        out_ref[r] = mm(to_slab, src).astype(BF16)
        return 0

    last.step3()
    lax.fori_loop(0, WH, out_row, 0)

    store(GROUPS - 1)
    home.wait_recv()

    def edge_row(r, _):
        rows = pl.ds(pl.multiple_of(r * WW, WW), WW)
        y = mm(edge_slab, back_ref[rows, :]).astype(BF16)
        out_ref[r, COLS - WW:, :] = out_ref[r, COLS - WW:, :] + y
        return 0

    lax.fori_loop(0, WH, edge_row, 0)

    pick = iota((16, C), 1) == 2 * (here.lon * 4 + here.lat) + iota((16, C), 0)
    w_rows = mm(one_hot(pick), wqkv_ref[...])[0:2]
    gain_rows = jnp.sum(jnp.where(pick, jnp.broadcast_to(gain, (16, C)), 0.0), axis=1, keepdims=True)[0:2]

    store(GROUPS)
    gg = jnp.sum(gq_ref[...] * w_rows, axis=1, keepdims=True) / gain_rows
    gg_ref[...] = jnp.where(iota((1, 2), 1) == 0, gg[0:1], gg[1:2])

    parts = split3(g4[...])
    total = mm(parts[0], hot[...], NT) + mm(parts[1], hot[...], NT) + mm(parts[2], hot[...], NT)
    gt_ref[...] = total[:, 0:NREL] * ((TOK * n_dev) // WIN) ** (-0.5)

    for piece in pieces:
        piece.finish()
    for copy in halo + [home]:
        copy.wait_send()


def piece_scratch(width):
    return [
        pltpu.VMEM((2, 4, 4, 16, width), BF16),
        pltpu.VMEM((4, 4, 16, width), BF16),
        pltpu.VMEM((4, 4, 16, width), BF16),
        pltpu.VMEM((3, 4, 16, width), BF16),
        pltpu.VMEM((4, 16, width), BF16),
        pltpu.VMEM((3, 16, width), BF16),
        pltpu.VMEM((NZ, 2, width), F32),
        pltpu.VMEM((NZ - 1, 2, width), F32),
        pltpu.SemaphoreType.DMA((14,)),
        pltpu.SemaphoreType.DMA((14,)),
    ]


def table_scratch(groups):
    counts = Reduction.counts
    return (
        [pltpu.VMEM((n, 16 * groups, 128), BF16) for n in counts]
        + [pltpu.SemaphoreType.DMA((n,)) for n in counts]
        + [pltpu.SemaphoreType.DMA((n,)) for n in counts]
    )


def fused(n_dev, *args):
    vm = pl.BlockSpec(memory_space=pltpu.VMEM)
    return pl.pallas_call(
        functools.partial(body, n_dev),
        out_shape=(
            jax.ShapeDtypeStruct((WH, COLS, C), BF16),
            jax.ShapeDtypeStruct((2, 3 * C), F32),
            jax.ShapeDtypeStruct((2, C), F32),
            jax.ShapeDtypeStruct((1, 2), F32),
            jax.ShapeDtypeStruct((H, NREL), F32),
        ),
        in_specs=[pl.BlockSpec(memory_space=pltpu.SMEM)] + [vm] * 7,
        out_specs=(vm,) * 5,
        scratch_shapes=[
            pltpu.VMEM((NWIN, WIN, C), BF16),
            pltpu.VMEM((NWIN, WIN, C), BF16),
            pltpu.VMEM((NWIN, WIN, C), F32),
            pltpu.VMEM((NWIN, WIN, 1), F32),
            pltpu.VMEM((NWIN, WIN, C), BF16),
            pltpu.VMEM((C, TOK), BF16),
            pltpu.VMEM((12, NWIN, WIN, 128), BF16),
            pltpu.VMEM((GROUPS, NWIN, WIN, 128), BF16),
            pltpu.VMEM((GROUPS, NWIN, WIN, 512), BF16),
            pltpu.VMEM((C, TOK), BF16),
            pltpu.VMEM((3, GROUPS, NWIN, WIN, 128), BF16),
            pltpu.VMEM((NWIN, WIN, C), F32),
            pltpu.VMEM((WIN, 512), F32),
            pltpu.VMEM((H, WIN, WIN), F32),
            pltpu.VMEM((512, 512), BF16),
            pltpu.VMEM((H, 512), F32),
            pltpu.VMEM((NWIN, WIN, C), BF16),
            pltpu.VMEM((C, TOK), BF16),
            pltpu.VMEM((WH, WW, C), BF16),
            pltpu.VMEM((WH, WW, C), BF16),
            pltpu.VMEM((WIN, C), BF16),
            pltpu.SemaphoreType.DMA((3,)),
            pltpu.SemaphoreType.DMA((3,)),
        ]
        + [ref for width in PIECES for ref in piece_scratch(width)]
        + [ref for groups in TABLE_GROUPS.values() for ref in table_scratch(len(groups))],
        compiler_params=pltpu.CompilerParams(
            vmem_limit_bytes=58 * 1024 * 1024, collective_id=0, has_side_effects=True
        ),
        name="fused",
    )(*args)


def handover_body(n, *refs):
    src, dst, hold = refs[:n], refs[n:2 * n], refs[2 * n:3 * n]
    sem_in, sem_out = refs[3 * n:]

    def route(a, m, b):
        rows = [(a[0].at[r], m[0].at[r], b[0].at[r]) for r in range(WH)]
        return rows + [(a[i], m[i], b[i]) for i in range(1, n)]

    hops = route(src, hold, dst)
    into = [pltpu.make_async_copy(a, m, sem_in.at[i]) for i, (a, m, _) in enumerate(hops)]
    out = [pltpu.make_async_copy(m, b, sem_out.at[i]) for i, (_, m, b) in enumerate(hops)]
    for copy in into:
        copy.start()
    for copy, then in zip(into, out):
        copy.wait()
        then.start()
    for copy in out:
        copy.wait()


def handover(*arrays):
    hbm = pl.BlockSpec(memory_space=pl.ANY)
    n = len(arrays)
    return pl.pallas_call(
        functools.partial(handover_body, n),
        out_shape=tuple(jax.ShapeDtypeStruct(a.shape, a.dtype) for a in arrays),
        in_specs=[hbm] * n,
        out_specs=(hbm,) * n,
        scratch_shapes=[pltpu.VMEM(a.shape, a.dtype) for a in arrays]
        + [pltpu.SemaphoreType.DMA((WH + n,)), pltpu.SemaphoreType.DMA((WH + n,))],
        name="handover",
    )(*arrays)


def shards(inputs, d_out, w_qkv, w_proj, gain, bias_table, rel_index, shifts):
    n_dev = lax.axis_size("lon") * lax.axis_size("lat")
    d_inputs, gq, gp, gg, gt = handover(*fused(
        n_dev, shifts, inputs, d_out, w_qkv, w_proj, gain.reshape(1, C), bias_table.T, rel_index
    ))
    return (d_inputs, gq, gp, gg.reshape(2), gt.T)


def solution(mesh):
    return jax.shard_map(
        shards,
        mesh=mesh,
        in_specs=(P("lat", "lon", None), P("lat", "lon", None), P(), P(), P(), P(), P(), P("lat")),
        out_specs=(
            P("lat", "lon", None),
            P(("lon", "lat"), None),
            P(("lon", "lat"), None),
            P(("lon", "lat")),
            P(),
        ),
        check_vma=False,
    )
```

```python
import functools

import jax
import jax.numpy as jnp
from jax import lax
from jax.experimental import pallas as pl
from jax.experimental.pallas import tpu as pltpu
from jax.sharding import PartitionSpec as P

C = 512
H = 16
HD = 32
WH = 8
WW = 16
WIN = 128
NREL = 465
COLS = 128
NWIN = 8
GROUPS = 4
TOK = NWIN * WIN
EPSILON = 1e-05
LOG2E = 1.4426950408889634
F32 = jnp.float32
BF16 = jnp.bfloat16

NN = (((1,), (0,)), ((), ()))
NT = (((1,), (1,)), ((), ()))


def mm(a, b, dims=NN):
    return lax.dot_general(a, b, dims, preferred_element_type=F32)


def iota(shape, dim):
    return lax.broadcasted_iota(jnp.int32, shape, dim)


def one_hot(cond):
    return jnp.where(cond, 1.0, 0.0).astype(BF16)


def split3(x):
    hi = x.astype(BF16)
    rest = x - hi.astype(F32)
    mid = rest.astype(BF16)
    low = (rest - mid.astype(F32)).astype(BF16)
    return hi, mid, low


def pair_masks(j):
    k = iota((WIN, WIN), 1)
    carry = (j % WW + k % WW) >= WW
    wrap = (j // WW + k // WW + carry.astype(jnp.int32)) >= WH
    return carry, wrap


def head_masks(rows):
    lane = iota((rows, 128), 1)
    return [(lane // HD) == h for h in range(4)]


NX, NY, NZ = 4, 4, 8
PIECES = (C, 384, 384, 384, 384)
TABLE_GROUPS = {3: (0, 1, 2), 4: (3,)}


class Place:
    def __init__(self):
        lon = lax.axis_index("lon")
        lat = lax.axis_index("lat")
        self.lon, self.lat = lon, lat
        self.core = lax.rem(lat, 2)
        self.x = (lon // 32) * 2 + lat // 2
        self.z = lax.rem(lon // 4, 8)
        self.y = lax.rem(lon, 4)
        self.a = self.x + self.core * (self.y - self.x)
        self.b = self.y + self.core * (self.x - self.y)

    def at(self, x=None, y=None, z=None, core=None):
        x = self.x if x is None else x
        y = self.y if y is None else y
        z = self.z if z is None else z
        core = self.core if core is None else core
        return ((x // 2) * 32 + z * 4 + y, lax.rem(x, 2) * 2 + core)

    def partner(self):
        return self.at(core=1 - self.core)

    def along(self, axis, step):
        if axis == "core":
            return self.partner()
        if axis in "ab":
            to_y = self.core if axis == "a" else 1 - self.core
            return self.at(
                x=lax.rem(self.x + (1 - to_y) * step, NX), y=lax.rem(self.y + to_y * step, NY)
            )
        return self.at(z=lax.rem(self.z + step, NZ))

    def slab(self, step):
        return (lax.rem(self.lon + 64 + step, 64), self.lat)


def remote(src, dst, send, recv, device):
    return pltpu.make_async_remote_copy(
        src_ref=src, dst_ref=dst, send_sem=send, recv_sem=recv,
        device_id=device, device_id_type=pl.DeviceIdType.MESH,
    )


class Reduction:
    axes = ("core", "a", "b", "z")
    counts = (2, 4, 4, NZ)

    def __init__(self, here, refs, table):
        self.here = here
        (self.s0, self.r0, self.s1, self.r1, self.s2, self.r2, self.s3, self.r3,
         self.send, self.recv) = refs
        self.table = table

    def copies(self, stage):
        here = self.here
        axis = self.axes[stage]
        out = []
        for step in range(1, self.counts[stage]):
            target = lax.rem(getattr(here, axis) + step, self.counts[stage])
            if stage == 0:
                src, dst = self.s0.at[target], self.r0
            elif stage == 1:
                src, dst = self.s1.at[target], self.r1.at[step - 1]
            elif stage == 2:
                src, dst = self.s2.at[target], self.r2.at[step - 1]
            else:
                src, dst = self.s3.at[target], self.r3.at[step - 1]
            slot = (0, 1, 4, 7)[stage] + step - 1
            out.append(
                remote(src, dst, self.send.at[slot], self.recv.at[slot], here.along(axis, step))
            )
        return out

    def table_copies(self, stage, arriving):
        if self.table is None:
            return []
        slots, send, recv = (part[stage] for part in self.table)
        axis = self.axes[stage]
        me = getattr(self.here, axis)
        out = []
        for step in range(1, self.counts[stage]):
            n = lax.rem(me + step, self.counts[stage]) if arriving else me
            out.append(
                remote(slots.at[me], slots.at[n], send.at[step], recv.at[n], self.here.along(axis, step))
            )
        return out

    def send_off(self, stage, table_value):
        for copy in self.copies(stage):
            copy.start()
        if self.table is not None:
            self.table[0][stage][getattr(self.here, self.axes[stage])] = table_value.astype(BF16)
            for copy in self.table_copies(stage, False):
                copy.start()

    def arrived(self, stage):
        for copy in self.copies(stage):
            copy.wait_recv()
        for copy in self.table_copies(stage, True):
            copy.wait_recv()
        if self.table is None:
            return None
        slots = self.table[0][stage]
        total = slots[0].astype(F32)
        for n in range(1, self.counts[stage]):
            total = total + slots[n].astype(F32)
        return total

    def start(self, table_value=None):
        self.send_off(0, table_value)

    def step1(self):
        table_value = self.arrived(0)
        for n in range(NX):
            own = self.s0[self.here.core, n].astype(F32)
            self.s1[n] = (own + self.r0[n].astype(F32)).astype(BF16)
        self.send_off(1, table_value)

    def step2(self):
        table_value = self.arrived(1)
        for n in range(4):
            total = self.s1[self.here.a, n].astype(F32)
            for r in range(3):
                total = total + self.r1[r, n].astype(F32)
            self.s2[n] = total.astype(BF16)
        self.send_off(2, table_value)

    def step3(self):
        table_value = self.arrived(2)
        total = self.s2[self.here.b].astype(F32)
        for r in range(3):
            total = total + self.r2[r].astype(F32)
        for z in range(NZ):
            self.s3[z] = total[2 * z:2 * z + 2]
        self.send_off(3, table_value)

    def step4(self):
        table_value = self.arrived(3)
        total = self.s3[self.here.z]
        for r in range(NZ - 1):
            total = total + self.r3[r]
        return total, table_value

    def finish(self):
        for stage in range(4):
            for copy in self.copies(stage) + self.table_copies(stage, False):
                copy.wait_send()


def body(
    n_dev,
    shift_ref, x_ref, d_ref, wqkv_ref, wproj_ref, gain_ref, table_ref, rel_ref,
    out_ref, gq_ref, gp_ref, gg_ref, gt_ref,
    xw, dw, nx, istd, normed, normed_t, qkv, dh, soft, att_t, dproj, dnorm, dsum, bias, hot, g4, ow, att_p,
    tx_ref, td_ref, back_ref, halo_send, halo_recv, *rest,
):
    here = Place()
    peers = [here.partner(), here.slab(1), here.slab(-1)]
    peers += [here.along("a", n) for n in range(1, NX)]
    peers += [here.along("b", n) for n in range(1, NY)]
    peers += [here.along("z", n) for n in range(1, NZ)]
    barrier = pltpu.get_barrier_semaphore()
    for peer in peers:
        pl.semaphore_signal(barrier, inc=1, device_id=peer, device_id_type=pl.DeviceIdType.MESH)
    pieces = []
    for p in range(len(PIECES)):
        refs = rest[p * 10:(p + 1) * 10]
        table = None
        if p in TABLE_GROUPS:
            base = len(PIECES) * 10 + 12 * list(TABLE_GROUPS).index(p)
            table = (rest[base:base + 4], rest[base + 4:base + 8], rest[base + 8:base + 12])
        pieces.append(Reduction(here, refs, table))

    s = shift_ref[0]
    w_i = iota((128, 128), 0)
    c_i = iota((128, 128), 1)
    to_win = one_hot(c_i == w_i - s)
    t_w = iota((16, 16), 0)
    t_c = iota((16, 16), 1)
    tail_win = one_hot(t_c == t_w - s + 16)
    gain = gain_ref[...]
    grad_scale = (TOK * n_dev) ** (-0.5)

    def shift_row(r, _):
        rows = pl.ds(pl.multiple_of(r * WW, WW), WW)
        for src, dst in ((x_ref, xw), (d_ref, dw)):
            y = mm(to_win, src[r]).astype(BF16)
            for w in range(NWIN):
                dst[w, rows, :] = y[w * WW:(w + 1) * WW]
        return 0

    lax.fori_loop(0, WH, shift_row, 0)

    pl.semaphore_wait(barrier, len(peers))

    edge = pl.ds(COLS - WW, WW)
    halo = [
        remote(src.at[:, edge, :], dst, halo_send.at[n], halo_recv.at[n], here.slab(1))
        for n, (src, dst) in enumerate(((x_ref, tx_ref), (d_ref, td_ref)))
    ]
    for copy in halo:
        copy.start()

    rel_t = rel_ref[...].astype(F32).T
    code_rows = []
    for wrap in (0, 1):
        for carry in (0, 1):
            j = 112 * wrap + 15 * carry
            row = rel_t[j:j + 1, :]
            code_rows.append(pltpu.roll(jnp.broadcast_to(row, (8, 128)), (128 - j) % 128, 1)[0:1])
    code = jnp.concatenate(code_rows, axis=1).astype(jnp.int32)
    hot[...] = one_hot(iota((512, 512), 0) == code)
    tab = jnp.concatenate([table_ref[...] * LOG2E, jnp.zeros((H, 512 - NREL), F32)], axis=1)
    parts = split3(tab)
    t4 = mm(parts[0], hot[...]) + mm(parts[1], hot[...]) + mm(parts[2], hot[...])
    g4[...] = t4
    carry_m, wrap_m = pair_masks(w_i)
    carry_r, wrap_r = pair_masks(127 - w_i)
    reverse = one_hot(w_i + c_i == 127)

    for h in range(H):
        row = [jnp.broadcast_to(g4[h:h + 1, q * 128:(q + 1) * 128], (128, 128)) for q in range(4)]
        base = jnp.where(
            wrap_m, jnp.where(carry_m, row[3], row[2]), jnp.where(carry_m, row[1], row[0])
        )
        bias[h] = pltpu.roll(base, 0, 1, stride=1, stride_axis=0)

    def norm_win(w, _):
        src = xw[w].astype(F32)
        mean = jnp.mean(src, axis=-1, keepdims=True)
        cen = src - mean
        inv = lax.rsqrt(jnp.mean(cen * cen, axis=-1, keepdims=True) + EPSILON)
        n = cen * inv
        nx[w] = n
        istd[w] = inv
        normed[w] = (n * gain).astype(BF16)
        return 0

    lax.fori_loop(2, NWIN, norm_win, 0)

    row_p = iota((C, C), 0)
    p_core, p_a, p_b = row_p // 256, (row_p // 64) % 4, (row_p // 16) % 4
    p_x = p_a + p_core * (p_b - p_a)
    p_y = p_b + p_core * (p_a - p_b)
    p_z, p_t = (row_p // 2) % 8, row_p % 2
    source = (p_x // 2) * 256 + p_z * 32 + p_y * 8 + (p_x % 2) * 4 + p_core * 2 + p_t
    order = one_hot(iota((C, C), 1) == source)

    def project(m, _):
        lhs = normed[pl.ds(2 * m, 2)].reshape(256, C)
        for n in range(3):
            y = mm(lhs, wqkv_ref[:, n * C:(n + 1) * C]).astype(BF16)
            for b in range(4):
                for ww in range(2):
                    qkv[n * 4 + b, 2 * m + ww] = y[ww * 128:(ww + 1) * 128, b * 128:(b + 1) * 128]
        y = mm(dw[pl.ds(2 * m, 2)].reshape(256, C), wproj_ref[...], NT).astype(BF16)
        for b in range(4):
            for ww in range(2):
                dh[b, 2 * m + ww] = y[ww * 128:(ww + 1) * 128, b * 128:(b + 1) * 128]
        normed_t[:, pl.ds(pl.multiple_of(m * 256, 256), 256)] = mm(order, lhs, NT).astype(BF16)
        return 0

    lax.fori_loop(1, 4, project, 0)
    masks = head_masks(128)

    def stack_heads(block):
        zero = jnp.zeros_like(block)
        return jnp.concatenate([jnp.where(m, block, zero) for m in masks], axis=0)

    def head_rows(block):
        cols = []
        for h in range(4):
            rows = [jnp.zeros((HD, block.shape[1]), block.dtype)] * 4
            rows[h] = block[h * HD:(h + 1) * HD]
            cols.append(jnp.concatenate(rows, axis=0))
        return jnp.concatenate(cols, axis=1)

    factor2 = HD ** (-0.5) * LOG2E

    def forward(blocks):
        scores = [mm(stack_heads(qkv[4 + g, w]), qkv[g, w], NT) for g, w in blocks]
        probs = [[] for _ in blocks]
        for h in range(4):
            for n, (g, _) in enumerate(blocks):
                z = scores[n][h * 128:(h + 1) * 128] * factor2 + bias[4 * g + h]
                e = jnp.exp2(z - jnp.max(z, axis=0, keepdims=True))
                probs[n].append((e * (1.0 / jnp.sum(e, axis=0, keepdims=True))).astype(BF16))
        for n, (g, w) in enumerate(blocks):
            stack = jnp.concatenate(probs[n], axis=0)
            soft[g, w] = stack
            rows = pl.ds(pl.multiple_of(g * 128, 128), 128)
            att_t[rows, w * WIN:(w + 1) * WIN] = mm(head_rows(qkv[8 + g, w].T), stack).astype(BF16)

    def fwd_step(g, _):
        forward([(g, w) for w in range(2, NWIN)])
        return 0

    lax.fori_loop(0, GROUPS, fwd_step, 0)

    for copy in halo:
        copy.wait_recv()

    def tail_row(r, _):
        rows = pl.ds(pl.multiple_of(r * WW, WW), WW)
        for src, dst in ((tx_ref, xw), (td_ref, dw)):
            y = mm(tail_win, src[r]).astype(BF16)
            dst[0, rows, :] = dst[0, rows, :] + y
        return 0

    lax.fori_loop(0, WH, tail_row, 0)
    lax.fori_loop(0, 2, norm_win, 0)
    project(0, 0)

    def fwd_late(i, _):
        forward([(2 * i + n, w) for n in range(2) for w in range(2)])
        return 0

    lax.fori_loop(0, GROUPS // 2, fwd_late, 0)

    def order_rows(m, _):
        cols = pl.ds(pl.multiple_of(m * 256, 256), 256)
        att_p[:, cols] = mm(order, att_t[:, cols]).astype(BF16)
        return 0

    lax.fori_loop(0, 4, order_rows, 0)

    def to_send(piece, y):
        y = (y * grad_scale).astype(BF16)
        for n in range(32):
            piece.s0[n // 16, (n // 4) % 4, n % 4] = y[n * 16:(n + 1) * 16]

    to_send(pieces[0], mm(att_p[...], dw[...].reshape(TOK, C)))
    pieces[0].start()

    factor = HD ** (-0.5)

    def backward(g, windows):
        grads = [mm(stack_heads(qkv[8 + g, w]), dh[g, w], NT) for w in windows]
        low = [[] for _ in windows]
        for h in range(4):
            hs = slice(h * 128, (h + 1) * 128)
            total = dsum[hs]
            for n, w in enumerate(windows):
                p = soft[g, w, hs].astype(F32)
                t = p * grads[n][hs]
                dsc = t - p * jnp.sum(t, axis=0, keepdims=True)
                total = total + dsc
                low[n].append(dsc.astype(BF16))
            dsum[hs] = total
        for n, w in enumerate(windows):
            wide = jnp.concatenate([soft[g, w, h * 128:(h + 1) * 128] for h in range(4)], axis=1)
            dv = mm(wide, stack_heads(dh[g, w]))
            dk = mm(jnp.concatenate(low[n], axis=1), stack_heads(qkv[g, w])) * factor
            dq = mm(head_rows(qkv[4 + g, w].T), jnp.concatenate(low[n], axis=0)) * factor
            dproj[0, g, w] = dq.astype(BF16).T
            dproj[1, g, w] = dk.astype(BF16)
            dproj[2, g, w] = dv.astype(BF16)

    def store(p):
        total, table_sum = pieces[p].step4()
        if p == 0:
            gp_ref[...] = total
        else:
            for b in range(3):
                gq_ref[:, b * C + (p - 1) * 128:b * C + p * 128] = total[:, b * 128:(b + 1) * 128]
        if p in TABLE_GROUPS:
            for n, group in enumerate(TABLE_GROUPS[p]):
                for h in range(4):
                    for q in range(4):
                        r = 16 * n + 4 * h + q
                        g4[4 * group + h:4 * group + h + 1, q * 128:(q + 1) * 128] = table_sum[r:r + 1]

    bias_sums = {}
    for g in range(GROUPS):
        dsum[...] = jnp.zeros_like(dsum)

        backward(g, range(0, 4))
        if g >= 3:
            store(g - 3)
        if g >= 2:
            pieces[g - 2].step3()
        pieces[g].step1()
        backward(g, range(4, 8))
        if g >= 1:
            pieces[g - 1].step2()

        sums = jnp.concatenate([dsum[h * 128:(h + 1) * 128] for h in range(4)], axis=1)
        flipped = sum(mm(reverse, part) for part in split3(sums))
        heads = bias_sums.setdefault(min(p for p in TABLE_GROUPS if g in TABLE_GROUPS[p]), [])
        for h in range(4):
            u = pltpu.roll(flipped[:, h * 128:(h + 1) * 128], 1, 1, stride=1, stride_axis=0)
            for q in range(4):
                keep = (wrap_r if q // 2 else ~wrap_r) & (carry_r if q % 2 else ~carry_r)
                heads.append(jnp.sum(jnp.where(keep, u, 0.0), axis=0, keepdims=True))

        grads = jnp.concatenate([dproj[b, g].reshape(TOK, 128) for b in range(3)], axis=1)
        to_send(pieces[g + 1], mm(normed_t[...], grads))
        pieces[g + 1].start(
            jnp.concatenate(bias_sums[g + 1], axis=0) if g + 1 in TABLE_GROUPS else None
        )

    def norm_grad(m, _):
        lhs = jnp.concatenate(
            [dproj[b, g, pl.ds(2 * m, 2)].reshape(256, 128) for b in range(3) for g in range(GROUPS)],
            axis=1,
        )
        dnorm[pl.ds(2 * m, 2)] = mm(lhs, wqkv_ref[...], NT).reshape(2, WIN, C)
        return 0

    last = pieces[GROUPS]

    def finish(w, _):
        n = nx[w]
        sc = dnorm[w] * gain
        m1 = jnp.mean(sc, axis=-1, keepdims=True)
        m2 = jnp.mean(sc * n, axis=-1, keepdims=True)
        branch = istd[w] * (sc - m1 - n * m2)
        ow[w] = (dw[w].astype(F32) + branch).astype(BF16)
        return 0

    norm_grad(0, 0)
    finish(0, 0)
    home = remote(ow.at[0], back_ref, halo_send.at[2], halo_recv.at[2], here.slab(-1))
    home.start()
    pieces[GROUPS - 2].step3()
    last.step1()
    norm_grad(1, 0)
    norm_grad(2, 0)
    pieces[GROUPS - 1].step2()
    norm_grad(3, 0)
    store(GROUPS - 3)
    lax.fori_loop(1, NWIN, finish, 0)
    store(GROUPS - 2)
    last.step2()
    pieces[GROUPS - 1].step3()

    to_slab = one_hot(c_i == w_i + s)
    edge_slab = one_hot(t_c == t_w + s - 16)

    def out_row(r, _):
        rows = pl.ds(pl.multiple_of(r * WW, WW), WW)
        src = jnp.concatenate([ow[w, rows, :] for w in range(NWIN)], axis=0)
        out_ref[r] = mm(to_slab, src).astype(BF16)
        return 0

    lax.fori_loop(0, WH, out_row, 0)

    home.wait_recv()

    def edge_row(r, _):
        rows = pl.ds(pl.multiple_of(r * WW, WW), WW)
        y = mm(edge_slab, back_ref[rows, :]).astype(BF16)
        out_ref[r, COLS - WW:, :] = out_ref[r, COLS - WW:, :] + y
        return 0

    lax.fori_loop(0, WH, edge_row, 0)
    last.step3()
    store(GROUPS - 1)

    pick = iota((16, C), 1) == 2 * (here.lon * 4 + here.lat) + iota((16, C), 0)
    w_rows = mm(one_hot(pick), wqkv_ref[...])[0:2]
    gain_rows = jnp.sum(jnp.where(pick, jnp.broadcast_to(gain, (16, C)), 0.0), axis=1, keepdims=True)[0:2]

    store(GROUPS)
    gg = jnp.sum(gq_ref[...] * w_rows, axis=1, keepdims=True) / gain_rows
    gg_ref[...] = jnp.where(iota((1, 2), 1) == 0, gg[0:1], gg[1:2])

    parts = split3(g4[...])
    total = mm(parts[0], hot[...], NT) + mm(parts[1], hot[...], NT) + mm(parts[2], hot[...], NT)
    gt_ref[...] = total[:, 0:NREL] * ((TOK * n_dev) // WIN) ** (-0.5)

    for piece in pieces:
        piece.finish()
    for copy in halo + [home]:
        copy.wait_send()


def piece_scratch(width):
    return [
        pltpu.VMEM((2, 4, 4, 16, width), BF16),
        pltpu.VMEM((4, 4, 16, width), BF16),
        pltpu.VMEM((4, 4, 16, width), BF16),
        pltpu.VMEM((3, 4, 16, width), BF16),
        pltpu.VMEM((4, 16, width), BF16),
        pltpu.VMEM((3, 16, width), BF16),
        pltpu.VMEM((NZ, 2, width), F32),
        pltpu.VMEM((NZ - 1, 2, width), F32),
        pltpu.SemaphoreType.DMA((14,)),
        pltpu.SemaphoreType.DMA((14,)),
    ]


def table_scratch(groups):
    counts = Reduction.counts
    return (
        [pltpu.VMEM((n, 16 * groups, 128), BF16) for n in counts]
        + [pltpu.SemaphoreType.DMA((n,)) for n in counts]
        + [pltpu.SemaphoreType.DMA((n,)) for n in counts]
    )


def fused(n_dev, *args):
    vm = pl.BlockSpec(memory_space=pltpu.VMEM)
    return pl.pallas_call(
        functools.partial(body, n_dev),
        out_shape=(
            jax.ShapeDtypeStruct((WH, COLS, C), BF16),
            jax.ShapeDtypeStruct((2, 3 * C), F32),
            jax.ShapeDtypeStruct((2, C), F32),
            jax.ShapeDtypeStruct((1, 2), F32),
            jax.ShapeDtypeStruct((H, NREL), F32),
        ),
        in_specs=[pl.BlockSpec(memory_space=pltpu.SMEM)] + [vm] * 7,
        out_specs=(vm,) * 5,
        scratch_shapes=[
            pltpu.VMEM((NWIN, WIN, C), BF16),
            pltpu.VMEM((NWIN, WIN, C), BF16),
            pltpu.VMEM((NWIN, WIN, C), F32),
            pltpu.VMEM((NWIN, WIN, 1), F32),
            pltpu.VMEM((NWIN, WIN, C), BF16),
            pltpu.VMEM((C, TOK), BF16),
            pltpu.VMEM((12, NWIN, WIN, 128), BF16),
            pltpu.VMEM((GROUPS, NWIN, WIN, 128), BF16),
            pltpu.VMEM((GROUPS, NWIN, 512, WIN), BF16),
            pltpu.VMEM((C, TOK), BF16),
            pltpu.VMEM((3, GROUPS, NWIN, WIN, 128), BF16),
            pltpu.VMEM((NWIN, WIN, C), F32),
            pltpu.VMEM((512, WIN), F32),
            pltpu.VMEM((H, WIN, WIN), F32),
            pltpu.VMEM((512, 512), BF16),
            pltpu.VMEM((H, 512), F32),
            pltpu.VMEM((NWIN, WIN, C), BF16),
            pltpu.VMEM((C, TOK), BF16),
            pltpu.VMEM((WH, WW, C), BF16),
            pltpu.VMEM((WH, WW, C), BF16),
            pltpu.VMEM((WIN, C), BF16),
            pltpu.SemaphoreType.DMA((3,)),
            pltpu.SemaphoreType.DMA((3,)),
        ]
        + [ref for width in PIECES for ref in piece_scratch(width)]
        + [ref for groups in TABLE_GROUPS.values() for ref in table_scratch(len(groups))],
        compiler_params=pltpu.CompilerParams(
            vmem_limit_bytes=58 * 1024 * 1024, collective_id=0, has_side_effects=True
        ),
        name="fused",
    )(*args)


def handover_body(n, *refs):
    src, dst, hold = refs[:n], refs[n:2 * n], refs[2 * n:3 * n]
    sem_in, sem_out = refs[3 * n:]

    def route(a, m, b):
        rows = [(a[0].at[r], m[0].at[r], b[0].at[r]) for r in range(WH)]
        return rows + [(a[i], m[i], b[i]) for i in range(1, n)]

    hops = route(src, hold, dst)
    into = [pltpu.make_async_copy(a, m, sem_in.at[i]) for i, (a, m, _) in enumerate(hops)]
    out = [pltpu.make_async_copy(m, b, sem_out.at[i]) for i, (_, m, b) in enumerate(hops)]
    for copy in into:
        copy.start()
    for copy, then in zip(into, out):
        copy.wait()
        then.start()
    for copy in out:
        copy.wait()


def handover(*arrays):
    hbm = pl.BlockSpec(memory_space=pl.ANY)
    n = len(arrays)
    return pl.pallas_call(
        functools.partial(handover_body, n),
        out_shape=tuple(jax.ShapeDtypeStruct(a.shape, a.dtype) for a in arrays),
        in_specs=[hbm] * n,
        out_specs=(hbm,) * n,
        scratch_shapes=[pltpu.VMEM(a.shape, a.dtype) for a in arrays]
        + [pltpu.SemaphoreType.DMA((WH + n,)), pltpu.SemaphoreType.DMA((WH + n,))],
        name="handover",
    )(*arrays)


def shards(inputs, d_out, w_qkv, w_proj, gain, bias_table, rel_index, shifts):
    n_dev = lax.axis_size("lon") * lax.axis_size("lat")
    d_inputs, gq, gp, gg, gt = handover(*fused(
        n_dev, shifts, inputs, d_out, w_qkv, w_proj, gain.reshape(1, C), bias_table.T, rel_index
    ))
    return (d_inputs, gq, gp, gg.reshape(2), gt.T)


def solution(mesh):
    return jax.shard_map(
        shards,
        mesh=mesh,
        in_specs=(P("lat", "lon", None), P("lat", "lon", None), P(), P(), P(), P(), P(), P("lat")),
        out_specs=(
            P("lat", "lon", None),
            P(("lon", "lat"), None),
            P(("lon", "lat"), None),
            P(("lon", "lat")),
            P(),
        ),
        check_vma=False,
    )
```

```python
import functools

import jax
import jax.numpy as jnp
from jax import lax
from jax.experimental import pallas as pl
from jax.experimental.pallas import tpu as pltpu
from jax.sharding import PartitionSpec as P

C = 512
H = 16
HD = 32
WH = 8
WW = 16
WIN = 128
NREL = 465
COLS = 128
NWIN = 8
GROUPS = 4
TOK = NWIN * WIN
EPSILON = 1e-05
LOG2E = 1.4426950408889634
F32 = jnp.float32
BF16 = jnp.bfloat16

NN = (((1,), (0,)), ((), ()))
NT = (((1,), (1,)), ((), ()))


def mm(a, b, dims=NN):
    return lax.dot_general(a, b, dims, preferred_element_type=F32)


def iota(shape, dim):
    return lax.broadcasted_iota(jnp.int32, shape, dim)


def one_hot(cond):
    return jnp.where(cond, 1.0, 0.0).astype(BF16)


def split3(x):
    hi = x.astype(BF16)
    rest = x - hi.astype(F32)
    mid = rest.astype(BF16)
    low = (rest - mid.astype(F32)).astype(BF16)
    return hi, mid, low


def pair_masks(j):
    k = iota((WIN, WIN), 1)
    carry = (j % WW + k % WW) >= WW
    wrap = (j // WW + k // WW + carry.astype(jnp.int32)) >= WH
    return carry, wrap


def head_masks(rows):
    lane = iota((rows, 128), 1)
    return [(lane // HD) == h for h in range(4)]


NX, NY, NZ = 4, 4, 8
PIECES = (C, 384, 384, 384, 384)
TABLE_GROUPS = {3: (0, 1, 2), 4: (3,)}


class Place:
    def __init__(self):
        lon = lax.axis_index("lon")
        lat = lax.axis_index("lat")
        self.lon, self.lat = lon, lat
        self.core = lax.rem(lat, 2)
        self.x = (lon // 32) * 2 + lat // 2
        self.z = lax.rem(lon // 4, 8)
        self.y = lax.rem(lon, 4)
        self.a = self.x + self.core * (self.y - self.x)
        self.b = self.y + self.core * (self.x - self.y)

    def at(self, x=None, y=None, z=None, core=None):
        x = self.x if x is None else x
        y = self.y if y is None else y
        z = self.z if z is None else z
        core = self.core if core is None else core
        return ((x // 2) * 32 + z * 4 + y, lax.rem(x, 2) * 2 + core)

    def partner(self):
        return self.at(core=1 - self.core)

    def along(self, axis, step):
        if axis == "core":
            return self.partner()
        if axis in "ab":
            to_y = self.core if axis == "a" else 1 - self.core
            return self.at(
                x=lax.rem(self.x + (1 - to_y) * step, NX), y=lax.rem(self.y + to_y * step, NY)
            )
        return self.at(z=lax.rem(self.z + step, NZ))

    def slab(self, step):
        return (lax.rem(self.lon + 64 + step, 64), self.lat)


def remote(src, dst, send, recv, device):
    return pltpu.make_async_remote_copy(
        src_ref=src, dst_ref=dst, send_sem=send, recv_sem=recv,
        device_id=device, device_id_type=pl.DeviceIdType.MESH,
    )


class Reduction:
    axes = ("core", "a", "b", "z")
    counts = (2, 4, 4, NZ)

    def __init__(self, here, refs, table):
        self.here = here
        (self.s0, self.r0, self.s1, self.r1, self.s2, self.r2, self.s3, self.r3,
         self.send, self.recv) = refs
        self.table = table

    def copies(self, stage):
        here = self.here
        axis = self.axes[stage]
        out = []
        for step in range(1, self.counts[stage]):
            target = lax.rem(getattr(here, axis) + step, self.counts[stage])
            if stage == 0:
                src, dst = self.s0.at[target], self.r0
            elif stage == 1:
                src, dst = self.s1.at[target], self.r1.at[step - 1]
            elif stage == 2:
                src, dst = self.s2.at[target], self.r2.at[step - 1]
            else:
                src, dst = self.s3.at[target], self.r3.at[step - 1]
            slot = (0, 1, 4, 7)[stage] + step - 1
            out.append(
                remote(src, dst, self.send.at[slot], self.recv.at[slot], here.along(axis, step))
            )
        return out

    def table_copies(self, stage, arriving):
        if self.table is None:
            return []
        slots, send, recv = (part[stage] for part in self.table)
        axis = self.axes[stage]
        me = getattr(self.here, axis)
        out = []
        for step in range(1, self.counts[stage]):
            n = lax.rem(me + step, self.counts[stage]) if arriving else me
            out.append(
                remote(slots.at[me], slots.at[n], send.at[step], recv.at[n], self.here.along(axis, step))
            )
        return out

    def send_off(self, stage, table_value):
        for copy in self.copies(stage):
            copy.start()
        if self.table is not None:
            self.table[0][stage][getattr(self.here, self.axes[stage])] = table_value.astype(BF16)
            for copy in self.table_copies(stage, False):
                copy.start()

    def arrived(self, stage):
        for copy in self.copies(stage):
            copy.wait_recv()
        for copy in self.table_copies(stage, True):
            copy.wait_recv()
        if self.table is None:
            return None
        slots = self.table[0][stage]
        total = slots[0].astype(F32)
        for n in range(1, self.counts[stage]):
            total = total + slots[n].astype(F32)
        return total

    def start(self, table_value=None):
        self.send_off(0, table_value)

    def step1(self):
        table_value = self.arrived(0)
        for n in range(NX):
            own = self.s0[self.here.core, n].astype(F32)
            self.s1[n] = (own + self.r0[n].astype(F32)).astype(BF16)
        self.send_off(1, table_value)

    def step2(self):
        table_value = self.arrived(1)
        for n in range(4):
            total = self.s1[self.here.a, n].astype(F32)
            for r in range(3):
                total = total + self.r1[r, n].astype(F32)
            self.s2[n] = total.astype(BF16)
        self.send_off(2, table_value)

    def step3(self):
        table_value = self.arrived(2)
        total = self.s2[self.here.b].astype(F32)
        for r in range(3):
            total = total + self.r2[r].astype(F32)
        for z in range(NZ):
            self.s3[z] = total[2 * z:2 * z + 2]
        self.send_off(3, table_value)

    def step4(self):
        table_value = self.arrived(3)
        total = self.s3[self.here.z]
        for r in range(NZ - 1):
            total = total + self.r3[r]
        return total, table_value

    def finish(self):
        for stage in range(4):
            for copy in self.copies(stage) + self.table_copies(stage, False):
                copy.wait_send()


def body(
    n_dev,
    shift_ref, x_ref, d_ref, wqkv_hbm, wproj_hbm, gain_ref, table_ref, rel_ref,
    out_ref, gq_ref, gp_ref, gg_ref, gt_ref,
    xw, dw, nx, istd, normed, normed_t, qkv, dh, soft, att_t, dproj, dnorm, dsum, bias, hot, g4, ow, att_p,
    tx_ref, td_ref, back_ref, halo_send, halo_recv, wqkv_ref, wproj_ref, weight_sem, *rest,
):
    here = Place()
    peers = [here.partner(), here.slab(1), here.slab(-1)]
    peers += [here.along("a", n) for n in range(1, NX)]
    peers += [here.along("b", n) for n in range(1, NY)]
    peers += [here.along("z", n) for n in range(1, NZ)]
    barrier = pltpu.get_barrier_semaphore()
    for peer in peers:
        pl.semaphore_signal(barrier, inc=1, device_id=peer, device_id_type=pl.DeviceIdType.MESH)
    pieces = []
    for p in range(len(PIECES)):
        refs = rest[p * 10:(p + 1) * 10]
        table = None
        if p in TABLE_GROUPS:
            base = len(PIECES) * 10 + 12 * list(TABLE_GROUPS).index(p)
            table = (rest[base:base + 4], rest[base + 4:base + 8], rest[base + 8:base + 12])
        pieces.append(Reduction(here, refs, table))

    weights = [
        pltpu.make_async_copy(src, dst, weight_sem.at[n])
        for n, (src, dst) in enumerate(((wqkv_hbm, wqkv_ref), (wproj_hbm, wproj_ref)))
    ]
    for copy in weights:
        copy.start()

    s = shift_ref[0]
    w_i = iota((128, 128), 0)
    c_i = iota((128, 128), 1)
    to_win = one_hot(c_i == w_i - s)
    t_w = iota((16, 16), 0)
    t_c = iota((16, 16), 1)
    tail_win = one_hot(t_c == t_w - s + 16)
    gain = gain_ref[...]
    grad_scale = (TOK * n_dev) ** (-0.5)

    def shift_row(r):
        rows = pl.ds(r * WW, WW)
        for src, dst in ((x_ref, xw), (d_ref, dw)):
            y = mm(to_win, src[r]).astype(BF16)
            for w in range(NWIN):
                dst[w, rows, :] = y[w * WW:(w + 1) * WW]

    for n in range(0, WH):
        shift_row(n)

    pl.semaphore_wait(barrier, len(peers))

    edge = pl.ds(COLS - WW, WW)
    halo = [
        remote(src.at[:, edge, :], dst, halo_send.at[n], halo_recv.at[n], here.slab(1))
        for n, (src, dst) in enumerate(((x_ref, tx_ref), (d_ref, td_ref)))
    ]
    for copy in halo:
        copy.start()

    rel_t = rel_ref[...].astype(F32).T
    code_rows = []
    for wrap in (0, 1):
        for carry in (0, 1):
            j = 112 * wrap + 15 * carry
            row = rel_t[j:j + 1, :]
            code_rows.append(pltpu.roll(jnp.broadcast_to(row, (8, 128)), (128 - j) % 128, 1)[0:1])
    code = jnp.concatenate(code_rows, axis=1).astype(jnp.int32)
    hot[...] = one_hot(iota((512, 512), 0) == code)
    tab = jnp.concatenate([table_ref[...] * LOG2E, jnp.zeros((H, 512 - NREL), F32)], axis=1)
    parts = split3(tab)
    t4 = mm(parts[0], hot[...]) + mm(parts[1], hot[...]) + mm(parts[2], hot[...])
    g4[...] = t4
    carry_m, wrap_m = pair_masks(w_i)
    carry_r, wrap_r = pair_masks(127 - w_i)
    reverse = one_hot(w_i + c_i == 127)

    for h in range(H):
        row = [jnp.broadcast_to(g4[h:h + 1, q * 128:(q + 1) * 128], (128, 128)) for q in range(4)]
        base = jnp.where(
            wrap_m, jnp.where(carry_m, row[3], row[2]), jnp.where(carry_m, row[1], row[0])
        )
        bias[h] = pltpu.roll(base, 0, 1, stride=1, stride_axis=0)

    def norm_win(w):
        src = xw[w].astype(F32)
        mean = jnp.mean(src, axis=-1, keepdims=True)
        cen = src - mean
        inv = lax.rsqrt(jnp.mean(cen * cen, axis=-1, keepdims=True) + EPSILON)
        n = cen * inv
        nx[w] = n
        istd[w] = inv
        normed[w] = (n * gain).astype(BF16)

    for n in range(2, NWIN):
        norm_win(n)

    row_p = iota((C, C), 0)
    p_core, p_a, p_b = row_p // 256, (row_p // 64) % 4, (row_p // 16) % 4
    p_x = p_a + p_core * (p_b - p_a)
    p_y = p_b + p_core * (p_a - p_b)
    p_z, p_t = (row_p // 2) % 8, row_p % 2
    source = (p_x // 2) * 256 + p_z * 32 + p_y * 8 + (p_x % 2) * 4 + p_core * 2 + p_t
    order = one_hot(iota((C, C), 1) == source)

    def project(m):
        lhs = normed[pl.ds(2 * m, 2)].reshape(256, C)
        for n in range(3):
            y = mm(lhs, wqkv_ref[:, n * C:(n + 1) * C]).astype(BF16)
            for b in range(4):
                for ww in range(2):
                    qkv[n * 4 + b, 2 * m + ww] = y[ww * 128:(ww + 1) * 128, b * 128:(b + 1) * 128]
        y = mm(dw[pl.ds(2 * m, 2)].reshape(256, C), wproj_ref[...], NT).astype(BF16)
        for b in range(4):
            for ww in range(2):
                dh[b, 2 * m + ww] = y[ww * 128:(ww + 1) * 128, b * 128:(b + 1) * 128]
        normed_t[:, pl.ds(m * 256, 256)] = mm(order, lhs, NT).astype(BF16)

    for copy in weights:
        copy.wait()
    for n in range(1, 4):
        project(n)
    masks = head_masks(128)

    def stack_heads(block):
        zero = jnp.zeros_like(block)
        return jnp.concatenate([jnp.where(m, block, zero) for m in masks], axis=0)

    def head_rows(block):
        cols = []
        for h in range(4):
            rows = [jnp.zeros((HD, block.shape[1]), block.dtype)] * 4
            rows[h] = block[h * HD:(h + 1) * HD]
            cols.append(jnp.concatenate(rows, axis=0))
        return jnp.concatenate(cols, axis=1)

    factor2 = HD ** (-0.5) * LOG2E

    def forward(blocks):
        scores = [mm(stack_heads(qkv[4 + g, w]), qkv[g, w], NT) for g, w in blocks]
        probs = [[] for _ in blocks]
        for h in range(4):
            for n, (g, _) in enumerate(blocks):
                z = scores[n][h * 128:(h + 1) * 128] * factor2 + bias[4 * g + h]
                e = jnp.exp2(z - jnp.max(z, axis=0, keepdims=True))
                probs[n].append((e * (1.0 / jnp.sum(e, axis=0, keepdims=True))).astype(BF16))
        for n, (g, w) in enumerate(blocks):
            stack = jnp.concatenate(probs[n], axis=0)
            soft[g, w] = stack
            rows = pl.ds(pl.multiple_of(g * 128, 128), 128)
            att_t[rows, w * WIN:(w + 1) * WIN] = mm(head_rows(qkv[8 + g, w].T), stack).astype(BF16)

    def fwd_step(g, _):
        forward([(g, w) for w in range(2, NWIN)])
        return 0

    lax.fori_loop(0, GROUPS, fwd_step, 0)

    for copy in halo:
        copy.wait_recv()

    def tail_row(r):
        rows = pl.ds(r * WW, WW)
        for src, dst in ((tx_ref, xw), (td_ref, dw)):
            y = mm(tail_win, src[r]).astype(BF16)
            dst[0, rows, :] = dst[0, rows, :] + y

    for n in range(0, WH):
        tail_row(n)
    for n in range(0, 2):
        norm_win(n)
    project(0)

    def fwd_late(i, _):
        forward([(2 * i + n, w) for n in range(2) for w in range(2)])
        return 0

    lax.fori_loop(0, GROUPS // 2, fwd_late, 0)

    def order_rows(m):
        cols = pl.ds(m * 256, 256)
        att_p[:, cols] = mm(order, att_t[:, cols]).astype(BF16)

    for n in range(0, 4):
        order_rows(n)

    def to_send(piece, rows_ref, other, table_value=None):
        for core in (1 - here.core, here.core):
            rows = pl.ds(pl.multiple_of(core * 256, 256), 256)
            y = (mm(rows_ref[rows, :], other) * grad_scale).astype(BF16)
            for n in range(16):
                piece.s0[core, n // 4, n % 4] = y[n * 16:(n + 1) * 16]
            if core is not here.core:
                piece.start(table_value)

    to_send(pieces[0], att_p, dw[...].reshape(TOK, C))

    factor = HD ** (-0.5)

    def backward(g, windows):
        grads = [mm(stack_heads(qkv[8 + g, w]), dh[g, w], NT) for w in windows]
        low = [[] for _ in windows]
        for h in range(4):
            hs = slice(h * 128, (h + 1) * 128)
            total = dsum[hs]
            for n, w in enumerate(windows):
                p = soft[g, w, hs].astype(F32)
                t = p * grads[n][hs]
                dsc = t - p * jnp.sum(t, axis=0, keepdims=True)
                total = total + dsc
                low[n].append(dsc.astype(BF16))
            dsum[hs] = total
        for n, w in enumerate(windows):
            wide = jnp.concatenate([soft[g, w, h * 128:(h + 1) * 128] for h in range(4)], axis=1)
            dv = mm(wide, stack_heads(dh[g, w]))
            dk = mm(jnp.concatenate(low[n], axis=1), stack_heads(qkv[g, w])) * factor
            dq = mm(head_rows(qkv[4 + g, w].T), jnp.concatenate(low[n], axis=0)) * factor
            dproj[0, g, w] = dq.astype(BF16).T
            dproj[1, g, w] = dk.astype(BF16)
            dproj[2, g, w] = dv.astype(BF16)

    def store(p):
        total, table_sum = pieces[p].step4()
        if p == 0:
            gp_ref[...] = total
        else:
            for b in range(3):
                gq_ref[:, b * C + (p - 1) * 128:b * C + p * 128] = total[:, b * 128:(b + 1) * 128]
        if p in TABLE_GROUPS:
            for n, group in enumerate(TABLE_GROUPS[p]):
                for h in range(4):
                    for q in range(4):
                        r = 16 * n + 4 * h + q
                        g4[4 * group + h:4 * group + h + 1, q * 128:(q + 1) * 128] = table_sum[r:r + 1]

    bias_sums = {}
    for g in range(GROUPS):
        dsum[...] = jnp.zeros_like(dsum)

        backward(g, range(0, 4))
        if g == 2:
            pieces[0].step2()
        if g == 3:
            pieces[1].step2()
            pieces[0].step3()
        backward(g, range(4, 8))
        pieces[g].step1()

        sums = jnp.concatenate([dsum[h * 128:(h + 1) * 128] for h in range(4)], axis=1)
        flipped = sum(mm(reverse, part) for part in split3(sums))
        heads = bias_sums.setdefault(min(p for p in TABLE_GROUPS if g in TABLE_GROUPS[p]), [])
        for h in range(4):
            u = pltpu.roll(flipped[:, h * 128:(h + 1) * 128], 1, 1, stride=1, stride_axis=0)
            for q in range(4):
                keep = (wrap_r if q // 2 else ~wrap_r) & (carry_r if q % 2 else ~carry_r)
                heads.append(jnp.sum(jnp.where(keep, u, 0.0), axis=0, keepdims=True))

        grads = jnp.concatenate([dproj[b, g].reshape(TOK, 128) for b in range(3)], axis=1)
        to_send(
            pieces[g + 1], normed_t, grads,
            jnp.concatenate(bias_sums[g + 1], axis=0) if g + 1 in TABLE_GROUPS else None,
        )

    def norm_grad(m):
        lhs = jnp.concatenate(
            [dproj[b, g, pl.ds(2 * m, 2)].reshape(256, 128) for b in range(3) for g in range(GROUPS)],
            axis=1,
        )
        dnorm[pl.ds(2 * m, 2)] = mm(lhs, wqkv_ref[...], NT).reshape(2, WIN, C)

    last = pieces[GROUPS]

    def finish(w):
        n = nx[w]
        sc = dnorm[w] * gain
        m1 = jnp.mean(sc, axis=-1, keepdims=True)
        m2 = jnp.mean(sc * n, axis=-1, keepdims=True)
        branch = istd[w] * (sc - m1 - n * m2)
        ow[w] = (dw[w].astype(F32) + branch).astype(BF16)

    norm_grad(0)
    finish(0)
    home = remote(ow.at[0], back_ref, halo_send.at[2], halo_recv.at[2], here.slab(-1))
    home.start()
    pieces[2].step2()
    last.step1()
    norm_grad(1)
    norm_grad(2)
    pieces[1].step3()
    store(0)
    norm_grad(3)
    for n in range(1, NWIN):
        finish(n)
    pieces[3].step2()
    pieces[2].step3()

    to_slab = one_hot(c_i == w_i + s)
    edge_slab = one_hot(t_c == t_w + s - 16)

    def out_row(r):
        rows = pl.ds(r * WW, WW)
        src = jnp.concatenate([ow[w, rows, :] for w in range(NWIN)], axis=0)
        out_ref[r] = mm(to_slab, src).astype(BF16)

    for n in range(0, WH):
        out_row(n)

    home.wait_recv()

    def edge_row(r):
        rows = pl.ds(r * WW, WW)
        y = mm(edge_slab, back_ref[rows, :]).astype(BF16)
        out_ref[r, COLS - WW:, :] = out_ref[r, COLS - WW:, :] + y

    for n in range(0, WH):
        edge_row(n)
    last.step2()
    store(1)
    pieces[3].step3()
    store(2)
    last.step3()
    store(3)

    pick = iota((16, C), 1) == 2 * (here.lon * 4 + here.lat) + iota((16, C), 0)
    w_rows = mm(one_hot(pick), wqkv_ref[...])[0:2]
    gain_rows = jnp.sum(jnp.where(pick, jnp.broadcast_to(gain, (16, C)), 0.0), axis=1, keepdims=True)[0:2]

    store(GROUPS)
    gg = jnp.sum(gq_ref[...] * w_rows, axis=1, keepdims=True) / gain_rows
    gg_ref[...] = jnp.where(iota((1, 2), 1) == 0, gg[0:1], gg[1:2])

    parts = split3(g4[...])
    total = mm(parts[0], hot[...], NT) + mm(parts[1], hot[...], NT) + mm(parts[2], hot[...], NT)
    gt_ref[...] = total[:, 0:NREL] * ((TOK * n_dev) // WIN) ** (-0.5)

    for piece in pieces:
        piece.finish()
    for copy in halo + [home]:
        copy.wait_send()


def piece_scratch(width):
    return [
        pltpu.VMEM((2, 4, 4, 16, width), BF16),
        pltpu.VMEM((4, 4, 16, width), BF16),
        pltpu.VMEM((4, 4, 16, width), BF16),
        pltpu.VMEM((3, 4, 16, width), BF16),
        pltpu.VMEM((4, 16, width), BF16),
        pltpu.VMEM((3, 16, width), BF16),
        pltpu.VMEM((NZ, 2, width), F32),
        pltpu.VMEM((NZ - 1, 2, width), F32),
        pltpu.SemaphoreType.DMA((14,)),
        pltpu.SemaphoreType.DMA((14,)),
    ]


def table_scratch(groups):
    counts = Reduction.counts
    return (
        [pltpu.VMEM((n, 16 * groups, 128), BF16) for n in counts]
        + [pltpu.SemaphoreType.DMA((n,)) for n in counts]
        + [pltpu.SemaphoreType.DMA((n,)) for n in counts]
    )


def fused(n_dev, *args):
    vm = pl.BlockSpec(memory_space=pltpu.VMEM)
    hbm = pl.BlockSpec(memory_space=pl.ANY)
    return pl.pallas_call(
        functools.partial(body, n_dev),
        out_shape=(
            jax.ShapeDtypeStruct((WH, COLS, C), BF16),
            jax.ShapeDtypeStruct((2, 3 * C), F32),
            jax.ShapeDtypeStruct((2, C), F32),
            jax.ShapeDtypeStruct((1, 2), F32),
            jax.ShapeDtypeStruct((H, NREL), F32),
        ),
        in_specs=[pl.BlockSpec(memory_space=pltpu.SMEM), vm, vm, hbm, hbm, vm, vm, vm],
        out_specs=(vm,) * 5,
        scratch_shapes=[
            pltpu.VMEM((NWIN, WIN, C), BF16),
            pltpu.VMEM((NWIN, WIN, C), BF16),
            pltpu.VMEM((NWIN, WIN, C), F32),
            pltpu.VMEM((NWIN, WIN, 1), F32),
            pltpu.VMEM((NWIN, WIN, C), BF16),
            pltpu.VMEM((C, TOK), BF16),
            pltpu.VMEM((12, NWIN, WIN, 128), BF16),
            pltpu.VMEM((GROUPS, NWIN, WIN, 128), BF16),
            pltpu.VMEM((GROUPS, NWIN, 512, WIN), BF16),
            pltpu.VMEM((C, TOK), BF16),
            pltpu.VMEM((3, GROUPS, NWIN, WIN, 128), BF16),
            pltpu.VMEM((NWIN, WIN, C), F32),
            pltpu.VMEM((512, WIN), F32),
            pltpu.VMEM((H, WIN, WIN), F32),
            pltpu.VMEM((512, 512), BF16),
            pltpu.VMEM((H, 512), F32),
            pltpu.VMEM((NWIN, WIN, C), BF16),
            pltpu.VMEM((C, TOK), BF16),
            pltpu.VMEM((WH, WW, C), BF16),
            pltpu.VMEM((WH, WW, C), BF16),
            pltpu.VMEM((WIN, C), BF16),
            pltpu.SemaphoreType.DMA((3,)),
            pltpu.SemaphoreType.DMA((3,)),
            pltpu.VMEM((C, 3 * C), BF16),
            pltpu.VMEM((C, C), BF16),
            pltpu.SemaphoreType.DMA((2,)),
        ]
        + [ref for width in PIECES for ref in piece_scratch(width)]
        + [ref for groups in TABLE_GROUPS.values() for ref in table_scratch(len(groups))],
        compiler_params=pltpu.CompilerParams(
            vmem_limit_bytes=58 * 1024 * 1024, collective_id=0, has_side_effects=True
        ),
        name="fused",
    )(*args)


def handover_body(n, *refs):
    src, dst, hold = refs[:n], refs[n:2 * n], refs[2 * n:3 * n]
    sem_in, sem_out = refs[3 * n:]

    def route(a, m, b):
        rows = [(a[0].at[r], m[0].at[r], b[0].at[r]) for r in range(WH)]
        return rows + [(a[i], m[i], b[i]) for i in range(1, n)]

    hops = route(src, hold, dst)
    into = [pltpu.make_async_copy(a, m, sem_in.at[i]) for i, (a, m, _) in enumerate(hops)]
    out = [pltpu.make_async_copy(m, b, sem_out.at[i]) for i, (_, m, b) in enumerate(hops)]
    for copy in into:
        copy.start()
    for copy, then in zip(into, out):
        copy.wait()
        then.start()
    for copy in out:
        copy.wait()


def handover(*arrays):
    hbm = pl.BlockSpec(memory_space=pl.ANY)
    n = len(arrays)
    return pl.pallas_call(
        functools.partial(handover_body, n),
        out_shape=tuple(jax.ShapeDtypeStruct(a.shape, a.dtype) for a in arrays),
        in_specs=[hbm] * n,
        out_specs=(hbm,) * n,
        scratch_shapes=[pltpu.VMEM(a.shape, a.dtype) for a in arrays]
        + [pltpu.SemaphoreType.DMA((WH + n,)), pltpu.SemaphoreType.DMA((WH + n,))],
        name="handover",
    )(*arrays)


def shards(inputs, d_out, w_qkv, w_proj, gain, bias_table, rel_index, shifts):
    n_dev = lax.axis_size("lon") * lax.axis_size("lat")
    d_inputs, gq, gp, gg, gt = handover(*fused(
        n_dev, shifts, inputs, d_out, w_qkv, w_proj, gain.reshape(1, C), bias_table.T, rel_index
    ))
    return (d_inputs, gq, gp, gg.reshape(2), gt.T)


def solution(mesh):
    return jax.shard_map(
        shards,
        mesh=mesh,
        in_specs=(P("lat", "lon", None), P("lat", "lon", None), P(), P(), P(), P(), P(), P("lat")),
        out_specs=(
            P("lat", "lon", None),
            P(("lon", "lat"), None),
            P(("lon", "lat"), None),
            P(("lon", "lat")),
            P(),
        ),
        check_vma=False,
    )
```

```python
import functools

import jax
import jax.numpy as jnp
from jax import lax
from jax.experimental import pallas as pl
from jax.experimental.pallas import tpu as pltpu
from jax.sharding import PartitionSpec as P

C = 512
H = 16
HD = 32
WH = 8
WW = 16
WIN = 128
NREL = 465
COLS = 128
NWIN = 8
GROUPS = 4
TOK = NWIN * WIN
EPSILON = 1e-05
LOG2E = 1.4426950408889634
F32 = jnp.float32
BF16 = jnp.bfloat16

NN = (((1,), (0,)), ((), ()))
NT = (((1,), (1,)), ((), ()))


def mm(a, b, dims=NN):
    return lax.dot_general(a, b, dims, preferred_element_type=F32)


def iota(shape, dim):
    return lax.broadcasted_iota(jnp.int32, shape, dim)


def one_hot(cond):
    return jnp.where(cond, 1.0, 0.0).astype(BF16)


def split3(x):
    hi = x.astype(BF16)
    rest = x - hi.astype(F32)
    mid = rest.astype(BF16)
    low = (rest - mid.astype(F32)).astype(BF16)
    return hi, mid, low


def pair_masks(j):
    k = iota((WIN, WIN), 1)
    carry = (j % WW + k % WW) >= WW
    wrap = (j // WW + k // WW + carry.astype(jnp.int32)) >= WH
    return carry, wrap


def head_masks(rows):
    lane = iota((rows, 128), 1)
    return [(lane // HD) == h for h in range(4)]


NX, NY, NZ = 4, 4, 8
PIECES = (C, 768, 768)
TABLE_GROUPS = {1: (0, 1), 2: (2, 3)}


class Place:
    def __init__(self):
        lon = lax.axis_index("lon")
        lat = lax.axis_index("lat")
        self.lon, self.lat = lon, lat
        self.core = lax.rem(lat, 2)
        self.x = (lon // 32) * 2 + lat // 2
        self.z = lax.rem(lon // 4, 8)
        self.y = lax.rem(lon, 4)
        self.a = self.x + self.core * (self.y - self.x)
        self.b = self.y + self.core * (self.x - self.y)

    def at(self, x=None, y=None, z=None, core=None):
        x = self.x if x is None else x
        y = self.y if y is None else y
        z = self.z if z is None else z
        core = self.core if core is None else core
        return ((x // 2) * 32 + z * 4 + y, lax.rem(x, 2) * 2 + core)

    def partner(self):
        return self.at(core=1 - self.core)

    def along(self, axis, step):
        if axis == "core":
            return self.partner()
        if axis in "ab":
            to_y = self.core if axis == "a" else 1 - self.core
            return self.at(
                x=lax.rem(self.x + (1 - to_y) * step, NX), y=lax.rem(self.y + to_y * step, NY)
            )
        return self.at(z=lax.rem(self.z + step, NZ))

    def slab(self, step):
        return (lax.rem(self.lon + 64 + step, 64), self.lat)


def remote(src, dst, send, recv, device):
    return pltpu.make_async_remote_copy(
        src_ref=src, dst_ref=dst, send_sem=send, recv_sem=recv,
        device_id=device, device_id_type=pl.DeviceIdType.MESH,
    )


class Reduction:
    axes = ("core", "a", "b", "z")
    counts = (2, 4, 4, NZ)

    def __init__(self, here, refs, table):
        self.here = here
        (self.s0, self.r0, self.s1, self.r1, self.s2, self.r2, self.s3, self.r3,
         self.send, self.recv) = refs
        self.table = table

    def copies(self, stage):
        here = self.here
        axis = self.axes[stage]
        out = []
        for step in range(1, self.counts[stage]):
            target = lax.rem(getattr(here, axis) + step, self.counts[stage])
            if stage == 0:
                src, dst = self.s0.at[target], self.r0
            elif stage == 1:
                src, dst = self.s1.at[target], self.r1.at[step - 1]
            elif stage == 2:
                src, dst = self.s2.at[target], self.r2.at[step - 1]
            else:
                src, dst = self.s3.at[target], self.r3.at[step - 1]
            slot = (0, 1, 4, 7)[stage] + step - 1
            out.append(
                remote(src, dst, self.send.at[slot], self.recv.at[slot], here.along(axis, step))
            )
        return out

    def table_copies(self, stage, arriving):
        if self.table is None:
            return []
        slots, send, recv = (part[stage] for part in self.table)
        axis = self.axes[stage]
        me = getattr(self.here, axis)
        out = []
        for step in range(1, self.counts[stage]):
            n = lax.rem(me + step, self.counts[stage]) if arriving else me
            out.append(
                remote(slots.at[me], slots.at[n], send.at[step], recv.at[n], self.here.along(axis, step))
            )
        return out

    def send_off(self, stage, table_value):
        for copy in self.copies(stage):
            copy.start()
        if self.table is not None:
            self.table[0][stage][getattr(self.here, self.axes[stage])] = table_value.astype(BF16)
            for copy in self.table_copies(stage, False):
                copy.start()

    def arrived(self, stage):
        for copy in self.copies(stage):
            copy.wait_recv()
        for copy in self.table_copies(stage, True):
            copy.wait_recv()
        if self.table is None:
            return None
        slots = self.table[0][stage]
        total = slots[0].astype(F32)
        for n in range(1, self.counts[stage]):
            total = total + slots[n].astype(F32)
        return total

    def start(self, table_value=None):
        self.send_off(0, table_value)

    def step1(self):
        table_value = self.arrived(0)
        for n in range(NX):
            own = self.s0[self.here.core, n].astype(F32)
            self.s1[n] = (own + self.r0[n].astype(F32)).astype(BF16)
        self.send_off(1, table_value)

    def step2(self):
        table_value = self.arrived(1)
        for n in range(4):
            total = self.s1[self.here.a, n].astype(F32)
            for r in range(3):
                total = total + self.r1[r, n].astype(F32)
            self.s2[n] = total.astype(BF16)
        self.send_off(2, table_value)

    def step3(self):
        table_value = self.arrived(2)
        total = self.s2[self.here.b].astype(F32)
        for r in range(3):
            total = total + self.r2[r].astype(F32)
        for z in range(NZ):
            self.s3[z] = total[2 * z:2 * z + 2]
        self.send_off(3, table_value)

    def step4(self):
        table_value = self.arrived(3)
        total = self.s3[self.here.z]
        for r in range(NZ - 1):
            total = total + self.r3[r]
        return total, table_value

    def finish(self):
        for stage in range(4):
            for copy in self.copies(stage) + self.table_copies(stage, False):
                copy.wait_send()


def body(
    n_dev,
    shift_ref, x_ref, d_ref, wqkv_hbm, wproj_hbm, gain_ref, table_ref, rel_ref,
    out_ref, gq_ref, gp_ref, gg_ref, gt_ref,
    xw, dw, nx, istd, normed, normed_t, qkv, dh, soft, att_t, dproj, dnorm, dsum, bias, hot, g4, ow, att_p,
    tx_ref, td_ref, back_ref, halo_send, halo_recv, wqkv_ref, wproj_ref, weight_sem, *rest,
):
    here = Place()
    peers = [here.partner(), here.slab(1), here.slab(-1)]
    peers += [here.along("a", n) for n in range(1, NX)]
    peers += [here.along("b", n) for n in range(1, NY)]
    peers += [here.along("z", n) for n in range(1, NZ)]
    barrier = pltpu.get_barrier_semaphore()
    for peer in peers:
        pl.semaphore_signal(barrier, inc=1, device_id=peer, device_id_type=pl.DeviceIdType.MESH)
    pieces = []
    for p in range(len(PIECES)):
        refs = rest[p * 10:(p + 1) * 10]
        table = None
        if p in TABLE_GROUPS:
            base = len(PIECES) * 10 + 12 * list(TABLE_GROUPS).index(p)
            table = (rest[base:base + 4], rest[base + 4:base + 8], rest[base + 8:base + 12])
        pieces.append(Reduction(here, refs, table))

    weights = [
        pltpu.make_async_copy(src, dst, weight_sem.at[n])
        for n, (src, dst) in enumerate(((wqkv_hbm, wqkv_ref), (wproj_hbm, wproj_ref)))
    ]
    for copy in weights:
        copy.start()

    s = shift_ref[0]
    w_i = iota((128, 128), 0)
    c_i = iota((128, 128), 1)
    to_win = one_hot(c_i == w_i - s)
    t_w = iota((16, 16), 0)
    t_c = iota((16, 16), 1)
    tail_win = one_hot(t_c == t_w - s + 16)
    gain = gain_ref[...]
    grad_scale = (TOK * n_dev) ** (-0.5)

    def shift_row(r):
        rows = pl.ds(r * WW, WW)
        for src, dst in ((x_ref, xw), (d_ref, dw)):
            y = mm(to_win, src[r]).astype(BF16)
            for w in range(NWIN):
                dst[w, rows, :] = y[w * WW:(w + 1) * WW]

    for n in range(0, WH):
        shift_row(n)

    pl.semaphore_wait(barrier, len(peers))

    edge = pl.ds(COLS - WW, WW)
    halo = [
        remote(src.at[:, edge, :], dst, halo_send.at[n], halo_recv.at[n], here.slab(1))
        for n, (src, dst) in enumerate(((x_ref, tx_ref), (d_ref, td_ref)))
    ]
    for copy in halo:
        copy.start()

    rel_t = rel_ref[...].astype(F32).T
    code_rows = []
    for wrap in (0, 1):
        for carry in (0, 1):
            j = 112 * wrap + 15 * carry
            row = rel_t[j:j + 1, :]
            code_rows.append(pltpu.roll(jnp.broadcast_to(row, (8, 128)), (128 - j) % 128, 1)[0:1])
    code = jnp.concatenate(code_rows, axis=1).astype(jnp.int32)
    hot[...] = one_hot(iota((512, 512), 0) == code)
    tab = jnp.concatenate([table_ref[...] * LOG2E, jnp.zeros((H, 512 - NREL), F32)], axis=1)
    parts = split3(tab)
    t4 = mm(parts[0], hot[...]) + mm(parts[1], hot[...]) + mm(parts[2], hot[...])
    g4[...] = t4
    carry_m, wrap_m = pair_masks(w_i)
    carry_r, wrap_r = pair_masks(127 - w_i)
    reverse = one_hot(w_i + c_i == 127)

    for h in range(H):
        row = [jnp.broadcast_to(g4[h:h + 1, q * 128:(q + 1) * 128], (128, 128)) for q in range(4)]
        base = jnp.where(
            wrap_m, jnp.where(carry_m, row[3], row[2]), jnp.where(carry_m, row[1], row[0])
        )
        bias[h] = pltpu.roll(base, 0, 1, stride=1, stride_axis=0)

    def norm_win(w):
        src = xw[w].astype(F32)
        mean = jnp.mean(src, axis=-1, keepdims=True)
        cen = src - mean
        inv = lax.rsqrt(jnp.mean(cen * cen, axis=-1, keepdims=True) + EPSILON)
        n = cen * inv
        nx[w] = n
        istd[w] = inv
        normed[w] = (n * gain).astype(BF16)

    for n in range(2, NWIN):
        norm_win(n)

    row_p = iota((C, C), 0)
    p_core, p_a, p_b = row_p // 256, (row_p // 64) % 4, (row_p // 16) % 4
    p_x = p_a + p_core * (p_b - p_a)
    p_y = p_b + p_core * (p_a - p_b)
    p_z, p_t = (row_p // 2) % 8, row_p % 2
    source = (p_x // 2) * 256 + p_z * 32 + p_y * 8 + (p_x % 2) * 4 + p_core * 2 + p_t
    order = one_hot(iota((C, C), 1) == source)

    def project(m):
        lhs = normed[pl.ds(2 * m, 2)].reshape(256, C)
        for n in range(3):
            y = mm(lhs, wqkv_ref[:, n * C:(n + 1) * C]).astype(BF16)
            for b in range(4):
                for ww in range(2):
                    qkv[n * 4 + b, 2 * m + ww] = y[ww * 128:(ww + 1) * 128, b * 128:(b + 1) * 128]
        y = mm(dw[pl.ds(2 * m, 2)].reshape(256, C), wproj_ref[...], NT).astype(BF16)
        for b in range(4):
            for ww in range(2):
                dh[b, 2 * m + ww] = y[ww * 128:(ww + 1) * 128, b * 128:(b + 1) * 128]
        normed_t[:, pl.ds(m * 256, 256)] = mm(order, lhs, NT).astype(BF16)

    for copy in weights:
        copy.wait()
    for n in range(1, 4):
        project(n)
    masks = head_masks(128)

    def stack_heads(block):
        zero = jnp.zeros_like(block)
        return jnp.concatenate([jnp.where(m, block, zero) for m in masks], axis=0)

    def head_rows(block):
        cols = []
        for h in range(4):
            rows = [jnp.zeros((HD, block.shape[1]), block.dtype)] * 4
            rows[h] = block[h * HD:(h + 1) * HD]
            cols.append(jnp.concatenate(rows, axis=0))
        return jnp.concatenate(cols, axis=1)

    factor2 = HD ** (-0.5) * LOG2E

    def forward(blocks):
        scores = [mm(stack_heads(qkv[4 + g, w]), qkv[g, w], NT) for g, w in blocks]
        probs = [[] for _ in blocks]
        for h in range(4):
            for n, (g, _) in enumerate(blocks):
                z = scores[n][h * 128:(h + 1) * 128] * factor2 + bias[4 * g + h]
                e = jnp.exp2(z - jnp.max(z, axis=0, keepdims=True))
                probs[n].append((e * (1.0 / jnp.sum(e, axis=0, keepdims=True))).astype(BF16))
        for n, (g, w) in enumerate(blocks):
            stack = jnp.concatenate(probs[n], axis=0)
            soft[g, w] = stack
            rows = pl.ds(pl.multiple_of(g * 128, 128), 128)
            att_t[rows, w * WIN:(w + 1) * WIN] = mm(head_rows(qkv[8 + g, w].T), stack).astype(BF16)

    def fwd_step(g, _):
        forward([(g, w) for w in range(2, NWIN)])
        return 0

    lax.fori_loop(0, GROUPS, fwd_step, 0)

    for copy in halo:
        copy.wait_recv()

    def tail_row(r):
        rows = pl.ds(r * WW, WW)
        for src, dst in ((tx_ref, xw), (td_ref, dw)):
            y = mm(tail_win, src[r]).astype(BF16)
            dst[0, rows, :] = dst[0, rows, :] + y

    for n in range(0, WH):
        tail_row(n)
    for n in range(0, 2):
        norm_win(n)
    project(0)

    def fwd_late(i, _):
        forward([(2 * i + n, w) for n in range(2) for w in range(2)])
        return 0

    lax.fori_loop(0, GROUPS // 2, fwd_late, 0)

    def order_rows(m):
        cols = pl.ds(m * 256, 256)
        att_p[:, cols] = mm(order, att_t[:, cols]).astype(BF16)

    for n in range(0, 4):
        order_rows(n)

    def to_send(piece, rows_ref, other, table_value=None):
        for core in (1 - here.core, here.core):
            rows = pl.ds(pl.multiple_of(core * 256, 256), 256)
            y = (mm(rows_ref[rows, :], other) * grad_scale).astype(BF16)
            for n in range(16):
                piece.s0[core, n // 4, n % 4] = y[n * 16:(n + 1) * 16]
            if core is not here.core:
                piece.start(table_value)

    to_send(pieces[0], att_p, dw[...].reshape(TOK, C))

    factor = HD ** (-0.5)

    def backward(g, windows):
        grads = [mm(stack_heads(qkv[8 + g, w]), dh[g, w], NT) for w in windows]
        low = [[] for _ in windows]
        for h in range(4):
            hs = slice(h * 128, (h + 1) * 128)
            total = dsum[hs]
            for n, w in enumerate(windows):
                p = soft[g, w, hs].astype(F32)
                t = p * grads[n][hs]
                dsc = t - p * jnp.sum(t, axis=0, keepdims=True)
                total = total + dsc
                low[n].append(dsc.astype(BF16))
            dsum[hs] = total
        for n, w in enumerate(windows):
            wide = jnp.concatenate([soft[g, w, h * 128:(h + 1) * 128] for h in range(4)], axis=1)
            dv = mm(wide, stack_heads(dh[g, w]))
            dk = mm(jnp.concatenate(low[n], axis=1), stack_heads(qkv[g, w])) * factor
            dq = mm(head_rows(qkv[4 + g, w].T), jnp.concatenate(low[n], axis=0)) * factor
            dproj[0, g, w] = dq.astype(BF16).T
            dproj[1, g, w] = dk.astype(BF16)
            dproj[2, g, w] = dv.astype(BF16)

    def store(p):
        total, table_sum = pieces[p].step4()
        if p == 0:
            gp_ref[...] = total
        else:
            for n, group in enumerate(TABLE_GROUPS[p]):
                for b in range(3):
                    k = (3 * n + b) * 128
                    gq_ref[:, b * C + group * 128:b * C + (group + 1) * 128] = total[:, k:k + 128]
        if p in TABLE_GROUPS:
            for n, group in enumerate(TABLE_GROUPS[p]):
                for h in range(4):
                    for q in range(4):
                        r = 16 * n + 4 * h + q
                        g4[4 * group + h:4 * group + h + 1, q * 128:(q + 1) * 128] = table_sum[r:r + 1]

    bias_sums = {}
    for g in range(GROUPS):
        dsum[...] = jnp.zeros_like(dsum)

        backward(g, range(0, 4))
        if g == 2:
            pieces[0].step2()
        backward(g, range(4, 8))
        if g == 0:
            pieces[0].step1()
        if g == 2:
            pieces[1].step1()
        if g == 3:
            pieces[0].step3()

        sums = jnp.concatenate([dsum[h * 128:(h + 1) * 128] for h in range(4)], axis=1)
        flipped = sum(mm(reverse, part) for part in split3(sums))
        heads = bias_sums.setdefault(min(p for p in TABLE_GROUPS if g in TABLE_GROUPS[p]), [])
        for h in range(4):
            u = pltpu.roll(flipped[:, h * 128:(h + 1) * 128], 1, 1, stride=1, stride_axis=0)
            for q in range(4):
                keep = (wrap_r if q // 2 else ~wrap_r) & (carry_r if q % 2 else ~carry_r)
                heads.append(jnp.sum(jnp.where(keep, u, 0.0), axis=0, keepdims=True))

        if g % 2:
            piece = (g + 1) // 2
            grads = jnp.concatenate(
                [dproj[b, k].reshape(TOK, 128) for k in (g - 1, g) for b in range(3)], axis=1
            )
            to_send(pieces[piece], normed_t, grads, jnp.concatenate(bias_sums[piece], axis=0))

    def norm_grad(m):
        lhs = jnp.concatenate(
            [dproj[b, g, pl.ds(2 * m, 2)].reshape(256, 128) for b in range(3) for g in range(GROUPS)],
            axis=1,
        )
        dnorm[pl.ds(2 * m, 2)] = mm(lhs, wqkv_ref[...], NT).reshape(2, WIN, C)

    last = pieces[2]

    def finish(w):
        n = nx[w]
        sc = dnorm[w] * gain
        m1 = jnp.mean(sc, axis=-1, keepdims=True)
        m2 = jnp.mean(sc * n, axis=-1, keepdims=True)
        branch = istd[w] * (sc - m1 - n * m2)
        ow[w] = (dw[w].astype(F32) + branch).astype(BF16)

    norm_grad(0)
    finish(0)
    home = remote(ow.at[0], back_ref, halo_send.at[2], halo_recv.at[2], here.slab(-1))
    home.start()
    last.step1()
    norm_grad(1)
    pieces[1].step2()
    norm_grad(2)
    norm_grad(3)
    store(0)
    for n in range(1, NWIN):
        finish(n)
    pieces[1].step3()

    to_slab = one_hot(c_i == w_i + s)
    edge_slab = one_hot(t_c == t_w + s - 16)

    def out_row(r):
        rows = pl.ds(r * WW, WW)
        src = jnp.concatenate([ow[w, rows, :] for w in range(NWIN)], axis=0)
        out_ref[r] = mm(to_slab, src).astype(BF16)

    for n in range(0, WH):
        out_row(n)

    home.wait_recv()

    def edge_row(r):
        rows = pl.ds(r * WW, WW)
        y = mm(edge_slab, back_ref[rows, :]).astype(BF16)
        out_ref[r, COLS - WW:, :] = out_ref[r, COLS - WW:, :] + y

    for n in range(0, WH):
        edge_row(n)
    last.step2()
    store(1)
    last.step3()

    pick = iota((16, C), 1) == 2 * (here.lon * 4 + here.lat) + iota((16, C), 0)
    w_rows = mm(one_hot(pick), wqkv_ref[...])[0:2]
    gain_rows = jnp.sum(jnp.where(pick, jnp.broadcast_to(gain, (16, C)), 0.0), axis=1, keepdims=True)[0:2]

    store(2)
    gg = jnp.sum(gq_ref[...] * w_rows, axis=1, keepdims=True) / gain_rows
    gg_ref[...] = jnp.where(iota((1, 2), 1) == 0, gg[0:1], gg[1:2])

    parts = split3(g4[...])
    total = mm(parts[0], hot[...], NT) + mm(parts[1], hot[...], NT) + mm(parts[2], hot[...], NT)
    gt_ref[...] = total[:, 0:NREL] * ((TOK * n_dev) // WIN) ** (-0.5)

    for piece in pieces:
        piece.finish()
    for copy in halo + [home]:
        copy.wait_send()


def piece_scratch(width):
    return [
        pltpu.VMEM((2, 4, 4, 16, width), BF16),
        pltpu.VMEM((4, 4, 16, width), BF16),
        pltpu.VMEM((4, 4, 16, width), BF16),
        pltpu.VMEM((3, 4, 16, width), BF16),
        pltpu.VMEM((4, 16, width), BF16),
        pltpu.VMEM((3, 16, width), BF16),
        pltpu.VMEM((NZ, 2, width), F32),
        pltpu.VMEM((NZ - 1, 2, width), F32),
        pltpu.SemaphoreType.DMA((14,)),
        pltpu.SemaphoreType.DMA((14,)),
    ]


def table_scratch(groups):
    counts = Reduction.counts
    return (
        [pltpu.VMEM((n, 16 * groups, 128), BF16) for n in counts]
        + [pltpu.SemaphoreType.DMA((n,)) for n in counts]
        + [pltpu.SemaphoreType.DMA((n,)) for n in counts]
    )


def fused(n_dev, *args):
    vm = pl.BlockSpec(memory_space=pltpu.VMEM)
    hbm = pl.BlockSpec(memory_space=pl.ANY)
    return pl.pallas_call(
        functools.partial(body, n_dev),
        out_shape=(
            jax.ShapeDtypeStruct((WH, COLS, C), BF16),
            jax.ShapeDtypeStruct((2, 3 * C), F32),
            jax.ShapeDtypeStruct((2, C), F32),
            jax.ShapeDtypeStruct((1, 2), F32),
            jax.ShapeDtypeStruct((H, NREL), F32),
        ),
        in_specs=[pl.BlockSpec(memory_space=pltpu.SMEM), vm, vm, hbm, hbm, vm, vm, vm],
        out_specs=(vm,) * 5,
        scratch_shapes=[
            pltpu.VMEM((NWIN, WIN, C), BF16),
            pltpu.VMEM((NWIN, WIN, C), BF16),
            pltpu.VMEM((NWIN, WIN, C), F32),
            pltpu.VMEM((NWIN, WIN, 1), F32),
            pltpu.VMEM((NWIN, WIN, C), BF16),
            pltpu.VMEM((C, TOK), BF16),
            pltpu.VMEM((12, NWIN, WIN, 128), BF16),
            pltpu.VMEM((GROUPS, NWIN, WIN, 128), BF16),
            pltpu.VMEM((GROUPS, NWIN, 512, WIN), BF16),
            pltpu.VMEM((C, TOK), BF16),
            pltpu.VMEM((3, GROUPS, NWIN, WIN, 128), BF16),
            pltpu.VMEM((NWIN, WIN, C), F32),
            pltpu.VMEM((512, WIN), F32),
            pltpu.VMEM((H, WIN, WIN), F32),
            pltpu.VMEM((512, 512), BF16),
            pltpu.VMEM((H, 512), F32),
            pltpu.VMEM((NWIN, WIN, C), BF16),
            pltpu.VMEM((C, TOK), BF16),
            pltpu.VMEM((WH, WW, C), BF16),
            pltpu.VMEM((WH, WW, C), BF16),
            pltpu.VMEM((WIN, C), BF16),
            pltpu.SemaphoreType.DMA((3,)),
            pltpu.SemaphoreType.DMA((3,)),
            pltpu.VMEM((C, 3 * C), BF16),
            pltpu.VMEM((C, C), BF16),
            pltpu.SemaphoreType.DMA((2,)),
        ]
        + [ref for width in PIECES for ref in piece_scratch(width)]
        + [ref for groups in TABLE_GROUPS.values() for ref in table_scratch(len(groups))],
        compiler_params=pltpu.CompilerParams(
            vmem_limit_bytes=58 * 1024 * 1024, collective_id=0, has_side_effects=True
        ),
        name="fused",
    )(*args)


def handover_body(n, *refs):
    src, dst, hold = refs[:n], refs[n:2 * n], refs[2 * n:3 * n]
    sem_in, sem_out = refs[3 * n:]

    def route(a, m, b):
        rows = [(a[0].at[r], m[0].at[r], b[0].at[r]) for r in range(WH)]
        return rows + [(a[i], m[i], b[i]) for i in range(1, n)]

    hops = route(src, hold, dst)
    into = [pltpu.make_async_copy(a, m, sem_in.at[i]) for i, (a, m, _) in enumerate(hops)]
    out = [pltpu.make_async_copy(m, b, sem_out.at[i]) for i, (_, m, b) in enumerate(hops)]
    for copy in into:
        copy.start()
    for copy, then in zip(into, out):
        copy.wait()
        then.start()
    for copy in out:
        copy.wait()


def handover(*arrays):
    hbm = pl.BlockSpec(memory_space=pl.ANY)
    n = len(arrays)
    return pl.pallas_call(
        functools.partial(handover_body, n),
        out_shape=tuple(jax.ShapeDtypeStruct(a.shape, a.dtype) for a in arrays),
        in_specs=[hbm] * n,
        out_specs=(hbm,) * n,
        scratch_shapes=[pltpu.VMEM(a.shape, a.dtype) for a in arrays]
        + [pltpu.SemaphoreType.DMA((WH + n,)), pltpu.SemaphoreType.DMA((WH + n,))],
        name="handover",
    )(*arrays)


def shards(inputs, d_out, w_qkv, w_proj, gain, bias_table, rel_index, shifts):
    n_dev = lax.axis_size("lon") * lax.axis_size("lat")
    d_inputs, gq, gp, gg, gt = handover(*fused(
        n_dev, shifts, inputs, d_out, w_qkv, w_proj, gain.reshape(1, C), bias_table.T, rel_index
    ))
    return (d_inputs, gq, gp, gg.reshape(2), gt.T)


def solution(mesh):
    return jax.shard_map(
        shards,
        mesh=mesh,
        in_specs=(P("lat", "lon", None), P("lat", "lon", None), P(), P(), P(), P(), P(), P("lat")),
        out_specs=(
            P("lat", "lon", None),
            P(("lon", "lat"), None),
            P(("lon", "lat"), None),
            P(("lon", "lat")),
            P(),
        ),
        check_vma=False,
    )
```
